256 devices in a mesh: ctx: 32 (over z, x_lo, core), head: 8 (over x_hi, y).
Axes of the slice: x: 4 (x_hi: 2, x_lo: 2; x = x_hi * 2 + x_lo), y: 4, z: 8, core: 2. Of those that a mesh axis runs over, the one named last changes fastest.
Arguments:
- queries: bfloat16 [16384, 2048], P('ctx', 'head'), may hold values from -24 to 24
- keys: bfloat16 [16384, 1024], P('ctx', 'head'), may hold values from -6 to 6
- values: bfloat16 [16384, 1024], P('ctx', 'head'), may hold values from -6 to 6
- out_weight: bfloat16 [128, 16, 4608], P(None, 'head'), may hold values from -0.125 to 0.125
- cotangent: bfloat16 [16384, 4608], P(('ctx', 'head')), may hold values from -3 to 3
Outputs:
- query_grad: float32 [16384, 2048], P('ctx', 'head')
- key_grad: float32 [16384, 1024], P('ctx', 'head')
- value_grad: float32 [16384, 1024], P('ctx', 'head')
- weight_grad: float32 [128, 16, 4608], P('ctx', 'head')
The draws below stay inside these ranges and needn't reach their ends.
All inputs are finite; a program needn't handle non-finite values.
Results may differ from the reference program's by a relative error of at most 0.02.
Values may be sent and summed in bfloat16 or wider, within the bound.
No kernel may reach another device: no remote copies, remote signals or barrier semaphores. Data moves between devices by JAX's collectives and lax.ppermute only.
A program may use at most 128 MiB of HBM per device.

```python
import math
import jax
import jax.numpy as jnp
from jax import lax

D = 4608
HQ = 16
HK = 8
HD = 128
WINDOW = 4096
TOK_DEV = 512
SPAN = 8
TOKENS = 16384


def draw_queries(key, part):
    first_key, second_key = jax.random.split(jax.random.fold_in(key, 17))
    base = jnp.clip(jax.random.normal(first_key, (TOKENS, HQ, HD), jnp.float32), -6.0, 6.0)
    scales = jnp.exp(jax.random.uniform(second_key, (TOKENS, HQ, 1), jnp.float32, math.log(0.5), math.log(4.0)))
    return (base * scales).reshape(TOKENS, HQ * HD).astype(jnp.bfloat16)


def level_of(rng, shape, pieces, least, high):
    def one(dim, blocks):
        draws = jax.random.uniform(jax.random.fold_in(jax.random.fold_in(rng, 6), dim), (blocks,), jnp.float32, least / len(pieces), high / len(pieces))
        return jnp.repeat(jnp.exp(draws), shape[dim] // blocks).reshape((-1,) + (1,) * (len(shape) - dim - 1))

    loudness = one(*pieces[0])
    for cut in pieces[1:]:
        loudness = loudness * one(*cut)
    return loudness


def gaussian(own_key, extent, spread, bound, cuts=(), held_as=jnp.bfloat16):
    values = spread * jax.random.normal(own_key, extent, jnp.float32)
    if cuts:
        values = values * level_of(own_key, extent, cuts, -0.22, 0.18)
    return jnp.clip(values, -bound, bound).astype(held_as)


def setup_inputs(seed: int = 0) -> dict:
    splits = jax.random.split(jax.random.key(seed), 6)
    queries = draw_queries(jax.random.fold_in(splits[5], 71), 0)
    keys = gaussian(splits[1], (TOKENS, HK * HD), 1.0, 6.0, ((0, 32), (1, 8)))
    values = gaussian(splits[2], (TOKENS, HK * HD), 1.0, 6.0, ((0, 32), (1, 8)))
    out_weight = gaussian(splits[3], (HD, HQ, D), (HQ * HD) ** -0.5, 0.125, ((1, 8),))
    cotangent = gaussian(splits[4], (TOKENS, D), 0.5, 3.0, ((0, 256),))
    return dict(queries=queries, keys=keys, values=values, out_weight=out_weight, cotangent=cotangent)


SOFT_CAP = 50.0
QUERY_MULTIPLIER = 144.0 ** -0.5
ROPE_BASE = 10000.0


def rotary_tables(positions, width):
    half_width = width // 2
    frequency = ROPE_BASE ** (-(jnp.arange(half_width, dtype=jnp.float32) * 2.0) / width)
    angles = positions.astype(jnp.float32)[:, None] * frequency[None, :]
    return jnp.cos(angles)[:, None, :], jnp.sin(angles)[:, None, :]


def rotate(values_in, cosine, sine_table):
    half_width = values_in.shape[-1] // 2
    first_half = values_in[..., :half_width]
    second_half = values_in[..., half_width:]
    return jnp.concatenate([first_half * cosine - second_half * sine_table, second_half * cosine + first_half * sine_table], axis=-1)


def unrotate(values_in, cosine, sine_table):
    half_width = values_in.shape[-1] // 2
    first_half = values_in[..., :half_width]
    second_half = values_in[..., half_width:]
    return jnp.concatenate([first_half * cosine + second_half * sine_table, second_half * cosine - first_half * sine_table], axis=-1)


def return_journey(values_in):
    return lax.optimization_barrier(values_in.astype(jnp.bfloat16)).astype(jnp.float32)


def reference(queries, keys, values, out_weight, cotangent):
    group_size = HQ // HK
    block = TOK_DEV
    blocks_all = TOKENS // block
    padding = SPAN * block
    width_keys = (SPAN + 1) * block
    positions = jnp.arange(TOKENS, dtype=jnp.int32)
    cosine, sine_table = rotary_tables(positions, HD)
    query_rotated = return_journey(rotate(queries.reshape(TOKENS, HQ, HD).astype(jnp.float32), cosine, sine_table)).reshape(TOKENS, HK, group_size, HD)
    key_rot = return_journey(rotate(keys.reshape(TOKENS, HK, HD).astype(jnp.float32), cosine, sine_table))
    value_all = values.reshape(TOKENS, HK, HD).astype(jnp.float32)
    output_gradient = return_journey(jnp.einsum("td,ehd->the", cotangent.astype(jnp.float32), out_weight.astype(jnp.float32))).reshape(TOKENS, HK, group_size, HD)
    key_pad = jnp.concatenate([jnp.zeros((padding, HK, HD), jnp.float32), key_rot], axis=0)
    value_pad = jnp.concatenate([jnp.zeros((padding, HK, HD), jnp.float32), value_all], axis=0)

    def one_block(state, block_index):
        key_grad_all, value_grad_all = state
        first = block_index * block
        query_block = lax.dynamic_slice_in_dim(query_rotated, first, block, 0)
        gradient_block = lax.dynamic_slice_in_dim(output_gradient, first, block, 0)
        key_window_rows = lax.dynamic_slice_in_dim(key_pad, first, width_keys, 0)
        value_window_rows = lax.dynamic_slice_in_dim(value_pad, first, width_keys, 0)
        query_pos = first + jnp.arange(block, dtype=jnp.int32)
        key_pos = first - padding + jnp.arange(width_keys, dtype=jnp.int32)
        offset = query_pos[:, None] - key_pos[None, :]
        visible = (offset >= 0) & (offset < WINDOW) & (key_pos[None, :] >= 0)
        uncapped_score = jnp.einsum("qfwy,vfy->fwqv", query_block, key_window_rows) * QUERY_MULTIPLIER
        tanh_val = jnp.tanh(uncapped_score / SOFT_CAP)
        capped = SOFT_CAP * tanh_val
        exponent_score = jnp.where(visible, jnp.exp(capped), 0.0)
        row_total = jnp.sum(exponent_score, axis=-1)
        weighted_values = jnp.einsum("fpxe,efv->xfpv", return_journey(exponent_score), value_window_rows)
        attn_blk = return_journey(weighted_values / jnp.transpose(row_total, (2, 0, 1))[..., None])
        log_total = jnp.log(row_total)
        row_delta = jnp.transpose(jnp.sum(gradient_block * attn_blk, axis=-1), (1, 2, 0))
        softmax_probability = jnp.where(visible, jnp.exp(capped - log_total[..., None]), 0.0)
        probability_gradient = jnp.einsum("qfwy,vfy->fwqv", gradient_block, value_window_rows)
        score_gradient = return_journey(softmax_probability * (probability_gradient - row_delta[..., None]) * (1.0 - tanh_val * tanh_val) * QUERY_MULTIPLIER)
        query_portion = jnp.einsum("fpxe,efv->xfpv", score_gradient, key_window_rows)
        key_portion = jnp.einsum("vcfh,fvcx->hvx", score_gradient, query_block)
        value_portion = jnp.einsum("vcfh,fvcx->hvx", return_journey(softmax_probability), gradient_block)
        key_grad_all = lax.dynamic_update_slice_in_dim(key_grad_all, lax.dynamic_slice_in_dim(key_grad_all, first, width_keys, 0) + key_portion, first, 0)
        value_grad_all = lax.dynamic_update_slice_in_dim(value_grad_all, lax.dynamic_slice_in_dim(value_grad_all, first, width_keys, 0) + value_portion, first, 0)
        return (key_grad_all, value_grad_all), (query_portion, attn_blk)

    start_state = (jnp.zeros((padding + TOKENS, HK, HD), jnp.float32), jnp.zeros((padding + TOKENS, HK, HD), jnp.float32))
    (key_grad_all, value_grad_all), (query_parts, attn_parts) = lax.scan(one_block, start_state, jnp.arange(blocks_all, dtype=jnp.int32))
    query_grad = unrotate(query_parts.reshape(TOKENS, HQ, HD), cosine, sine_table).reshape(TOKENS, HQ * HD)
    key_grad = unrotate(key_grad_all[padding:], cosine, sine_table).reshape(TOKENS, HK * HD)
    value_grad = value_grad_all[padding:].reshape(TOKENS, HK * HD)
    attn_all = attn_parts.reshape(TOKENS, HQ, HD)
    weight_grad = jnp.einsum("the,td->ehd", attn_all, cotangent.astype(jnp.float32))
    return (query_grad, key_grad, value_grad, weight_grad)
```

```python
import jax
import jax.numpy as jnp
from jax import lax
from jax.experimental import pallas as pl
from jax.experimental.pallas import tpu as pltpu
from jax.sharding import Mesh, PartitionSpec as P

SOFT_CAP = 50.0
QUERY_MULTIPLIER = 144.0 ** (-0.5)
ROPE_BASE = 10000.0
LOG2E = 1.4426950408889634
CTX = ("z", "xl", "c")
HEAD = ("xh", "y")
TOK = 512
HALF = 256
HD = 128
PANELS = 3
SLOTS = 12
TILES = 9
NT = (((1,), (1,)), ((), ()))
F32 = jnp.float32
BF16 = jnp.bfloat16


def permute(x, axis, pairs):
    return lax.ppermute(x, axis, pairs)


def from_y(x, d):
    return permute(x, "y", [((i + d) % 4, i) for i in range(4)])


def swap(x, axis):
    return permute(x, axis, [(0, 1), (1, 0)])


def along_z(x, step):
    return permute(x, "z", [(i, i + step) for i in range(8) if 0 <= i + step < 8])


def tables(first_row):
    half = HD // 2
    positions = first_row + jnp.arange(TOK, dtype=jnp.int32)
    frequency = ROPE_BASE ** (-(jnp.arange(half, dtype=F32) * 2.0) / HD)
    angles = positions.astype(F32)[:, None] * frequency[None, :]
    return jnp.cos(angles), jnp.sin(angles)


def ndot(a, b):
    return jnp.dot(a, b, preferred_element_type=F32)


def tdot(a, b):
    return lax.dot_general(a, b, NT, preferred_element_type=F32)


def forward_kernel(slot, tile, flag, q_ref, cos_ref, sin_ref, r0, r2, r1, r3, e_ref, g_ref, qr_ref, at_ref, li_ref, kv_ref, pt_ref, acc):
    step = pl.program_id(0)

    @pl.when(step == 0)
    def _():
        for n, ref in enumerate((r0, r2, r1, r3)):
            kv_ref[n * PANELS : (n + 1) * PANELS] = ref[...]
        acc[...] = jnp.zeros_like(acc)
        cosine = cos_ref[...]
        sine = sin_ref[...]
        for h in range(2):
            x = q_ref[:, h * HD : (h + 1) * HD].astype(F32)
            qr_ref[:, h * HD : (h + 1) * HD] = (x * cosine + pltpu.roll(x, HD // 2, 1) * sine).astype(BF16)

    def body(mode):
        key = kv_ref[slot[step], 0]
        value = jnp.concatenate([kv_ref[slot[step], 1], jnp.ones((TOK, HD), BF16)], axis=1)
        rows = HALF
        for h in range(2):
            for part in range(TOK // rows):
                at = pl.ds(part * rows, rows)
                s = tdot(qr_ref[at, h * HD : (h + 1) * HD], key)
                th = jnp.tanh(s * (QUERY_MULTIPLIER / SOFT_CAP))
                ex = jnp.exp2(th * (SOFT_CAP * LOG2E))
                if mode:
                    t = lax.broadcasted_iota(jnp.int32, (rows, TOK), 0) + part * rows
                    u = lax.broadcasted_iota(jnp.int32, (rows, TOK), 1)
                    ex = jnp.where(u > t if mode == 1 else u <= t, ex, 0.0)
                eb = ex.astype(BF16)
                e_ref[0, h, at, :] = eb
                g_ref[0, h, at, :] = (ex * (1.0 - th * th)).astype(BF16)
                acc[h, at, :] += ndot(eb, value)

    @pl.when(flag[step] == 1)
    def _():
        body(1)

    @pl.when(flag[step] == 2)
    def _():
        body(2)

    @pl.when(flag[step] == 3)
    def _():
        body(0)

    @pl.when(step == SLOTS - 1)
    def _():
        for h in range(2):
            inverse = 1.0 / acc[h, :, HD:]
            at_ref[:, h * HD : (h + 1) * HD] = (acc[h, :, :HD] * inverse).astype(BF16)
            li_ref[:, h * HD : (h + 1) * HD] = inverse
        row = lax.broadcasted_iota(jnp.int32, (2 * HD, 2 * HD), 0)
        col = lax.broadcasted_iota(jnp.int32, (2 * HD, 2 * HD), 1)
        core, left, plane, four, head = row // 128, (row // 64) % 2, (row // 8) % 8, (row // 2) % 4, row % 2
        source = head * HD + plane * 16 + left * 8 + core * 4 + four
        pick = jnp.where(col == source, 1.0, 0.0).astype(BF16)
        pt_ref[...] = tdot(pick, at_ref[...]).astype(BF16)


def forward(slot, tile, flag, queries, cosf, sinf, panels):
    whole = lambda *shape: pl.BlockSpec(shape, lambda i, *_: (0,) * len(shape))
    sds = jax.ShapeDtypeStruct
    eg = pl.BlockSpec((1, 2, TOK, TOK), lambda i, s, t, f: (t[i], 0, 0, 0))
    return pl.pallas_call(
        forward_kernel,
        out_shape=(
            sds((TILES, 2, TOK, TOK), BF16),
            sds((TILES, 2, TOK, TOK), BF16),
            sds((TOK, 2 * HD), BF16),
            sds((TOK, 2 * HD), BF16),
            sds((TOK, 2 * HD), F32),
            sds((SLOTS, 2, TOK, HD), BF16),
            sds((2 * HD, TOK), BF16),
        ),
        grid_spec=pltpu.PrefetchScalarGridSpec(
            num_scalar_prefetch=3,
            grid=(SLOTS,),
            in_specs=[
                whole(TOK, 2 * HD),
                whole(TOK, HD),
                whole(TOK, HD),
                *([whole(PANELS, 2, TOK, HD)] * 4),
            ],
            out_specs=(
                eg,
                eg,
                whole(TOK, 2 * HD),
                whole(TOK, 2 * HD),
                whole(TOK, 2 * HD),
                whole(SLOTS, 2, TOK, HD),
                whole(2 * HD, TOK),
            ),
            scratch_shapes=[pltpu.VMEM((2, TOK, 2 * HD), F32)],
        ),
        compiler_params=pltpu.CompilerParams(dimension_semantics=("arbitrary",), vmem_limit_bytes=60 << 20),
        cost_estimate=pl.CostEstimate(flops=10_000_000_000, bytes_accessed=24_000_000, transcendentals=10_000_000),
        name="attend",
    )(slot, tile, flag, queries, cosf, sinf, *panels)


def backward_kernel(last, *refs):
    slot, _, flag, where = refs[:4]
    c0, c1, c2, c3, w_ref, q_ref, at_ref, li_ref, cos_ref, sin_ref, kv_ref, e_ref, g_ref = refs[4:17]
    rest = refs[17:]
    if last:
        prev_ref, _, keep_ref, send_ref, qg_ref = rest[:5]
    else:
        part_ref, qg_ref = rest[:2]
    cs, do, dl, qt, dt, dq = rest[-6:]
    step = pl.program_id(0)

    @pl.when(step == 0)
    def _():
        y = where[0]
        for d, ref in enumerate((c0, c1, c2, c3)):
            row = pl.multiple_of(lax.rem(y + d, 4) * 64, 64)
            cs[pl.ds(row, 64), :] = ref[...]
        do[...] = tdot(cs[...], w_ref[...]).astype(BF16)
        for h in range(2):
            col = slice(h * HD, (h + 1) * HD)
            grad = do[:, col].astype(F32)
            inverse = li_ref[:, col]
            total = jnp.sum(grad * at_ref[:, col].astype(F32), axis=1, keepdims=True)
            dl[h] = jnp.broadcast_to(total, (HALF, HD))
            dt[h] = (grad * inverse).T.astype(BF16)
            qt[h] = (q_ref[:, col].astype(F32) * (inverse * QUERY_MULTIPLIER)).T.astype(BF16)
        dq[...] = jnp.zeros_like(dq)

    @pl.when(flag[step] > 0)
    def _():
        key = kv_ref[0, 0]
        value = kv_ref[0, 1]
        dk = jnp.zeros((HD, TOK), F32)
        dv = jnp.zeros((HD, TOK), F32)
        for h in range(2):
            dp = tdot(do[:, h * HD : (h + 1) * HD], value)
            x = (g_ref[0, h].astype(F32) * (dp - dl[h][:, :1])).astype(BF16)
            dq[h] += ndot(x, key)
            dk += ndot(qt[h], x)
            dv += ndot(dt[h], e_ref[0, h])
        if last:
            dk = (dk + prev_ref[0, 0]).astype(BF16)
            dv = (dv + prev_ref[0, 1]).astype(BF16)
            at = slot[step]

            @pl.when(at < 6)
            def _():
                keep_ref[at, 0] = dk
                keep_ref[at, 1] = dv

            @pl.when(at >= 6)
            def _():
                send_ref[at - 6, 0] = dk
                send_ref[at - 6, 1] = dv
        else:
            part_ref[0, 0] = dk
            part_ref[0, 1] = dv

    if last:

        @pl.when(flag[step] == 0)
        def _():
            at = slot[step]
            zero = jnp.zeros((2, HD, TOK), BF16)

            @pl.when(at < 6)
            def _():
                keep_ref[at] = zero

            @pl.when(at >= 6)
            def _():
                send_ref[at - 6] = zero

    @pl.when(step == SLOTS - 1)
    def _():
        cosine = cos_ref[...]
        sine = sin_ref[...]
        for h in range(2):
            col = slice(h * HD, (h + 1) * HD)
            g = dq[h] * (li_ref[:, col] * QUERY_MULTIPLIER)
            qg_ref[:, col] = g * cosine - pltpu.roll(g, HD // 2, 1) * sine


def backward(slot, tile, flag, where, cots, w2, qr, attn, linv, cosf, sinf, kv, e, g, before):
    last = before is not None
    sds = jax.ShapeDtypeStruct
    whole = lambda *shape: pl.BlockSpec(shape, lambda i, *_: (0,) * len(shape))
    tok = lambda width: pl.BlockSpec((HALF, width), lambda i, s, t, f, w: (w[1], 0))
    eg = pl.BlockSpec((1, 2, HALF, TOK), lambda i, s, t, f, w: (t[i], 0, w[1], 0))
    part = pl.BlockSpec((1, 2, HD, TOK), lambda i, s, t, f, w: (s[i], 0, 0, 0))
    ins = [whole(64, 4608)] * 4 + [
        whole(2 * HD, 4608),
        tok(2 * HD),
        tok(2 * HD),
        tok(2 * HD),
        tok(HD),
        tok(HD),
        pl.BlockSpec((1, 2, TOK, HD), lambda i, s, t, f, w: (s[i], 0, 0, 0)),
        eg,
        eg,
    ]
    args = [*cots, w2, qr, attn, linv, cosf, sinf, kv, e, g]
    alias = {}
    if last:
        ins += [part, pl.BlockSpec(memory_space=pl.ANY)]
        args += list(before)
        outs = (whole(6, 2, HD, TOK), whole(6, 2, HD, TOK), tok(2 * HD))
        shapes = (sds((6, 2, HD, TOK), BF16), sds((6, 2, HD, TOK), BF16), sds((TOK, 2 * HD), F32))
        alias = {4 + len(args) - 1: 2}
    else:
        outs = (part, tok(2 * HD))
        shapes = (sds((SLOTS, 2, HD, TOK), F32), sds((TOK, 2 * HD), F32))

    def kernel(*refs):
        backward_kernel(last, *refs)

    return pl.pallas_call(
        kernel,
        out_shape=shapes,
        grid_spec=pltpu.PrefetchScalarGridSpec(
            num_scalar_prefetch=4,
            grid=(SLOTS,),
            in_specs=ins,
            out_specs=outs,
            scratch_shapes=[
                pltpu.VMEM((HALF, 4608), BF16),
                pltpu.VMEM((HALF, 2 * HD), BF16),
                pltpu.VMEM((2, HALF, HD), F32),
                pltpu.VMEM((2, HD, HALF), BF16),
                pltpu.VMEM((2, HD, HALF), BF16),
                pltpu.VMEM((2, HALF, HD), F32),
            ],
        ),
        compiler_params=pltpu.CompilerParams(dimension_semantics=("arbitrary",), vmem_limit_bytes=60 << 20),
        input_output_aliases=alias,
        cost_estimate=pl.CostEstimate(flops=8_000_000_000, bytes_accessed=24_000_000, transcendentals=0),
        name="pull_last" if last else "pull_first",
    )(slot, tile, flag, where, *args)


def weight_kernel(where, *refs):
    cots = refs[:8]
    at_ref, keep_ref, send_ref, cs = refs[8:]
    y, own, core = where[0], where[1], where[2]
    for n, ref in enumerate(cots):
        base = own if n < 4 else 1 - own
        row = pl.multiple_of(base * HALF + lax.rem(y + n % 4, 4) * 64, 64)
        cs[pl.ds(row, 64), :] = ref[...]
    rows = cs[...]
    mine = pl.multiple_of(core * HD, HD)
    other = pl.multiple_of((1 - core) * HD, HD)
    keep_ref[...] = ndot(at_ref[pl.ds(mine, HD), :], rows)
    send_ref[...] = ndot(at_ref[pl.ds(other, HD), :], rows).astype(BF16)


def weight(where, cots, attn_t):
    chunk = 512
    sds = jax.ShapeDtypeStruct
    block = lambda rows: pl.BlockSpec((rows, chunk), lambda i, w: (0, i))
    return pl.pallas_call(
        weight_kernel,
        out_shape=(sds((HD, 4608), F32), sds((HD, 4608), BF16)),
        grid_spec=pltpu.PrefetchScalarGridSpec(
            num_scalar_prefetch=1,
            grid=(4608 // chunk,),
            in_specs=[block(64)] * 8 + [pl.BlockSpec((2 * HD, TOK), lambda i, w: (0, 0))],
            out_specs=(block(HD), block(HD)),
            scratch_shapes=[pltpu.VMEM((TOK, chunk), BF16)],
        ),
        compiler_params=pltpu.CompilerParams(dimension_semantics=("arbitrary",), vmem_limit_bytes=60 << 20),
        cost_estimate=pl.CostEstimate(flops=1_300_000_000, bytes_accessed=9_000_000, transcendentals=0),
        name="weigh",
    )(where, *cots, attn_t)


def local(queries, keys, values, out_weight, cotangent):
    z, xl, c = (lax.axis_index(a) for a in CTX)
    xh, y = (lax.axis_index(a) for a in HEAD)
    lane = xl * 2 + c
    ctx = z * 4 + lane
    cosine, sine = tables(ctx * TOK)
    kf = keys.astype(F32)
    k1, k2 = kf[:, : HD // 2], kf[:, HD // 2 :]
    key_rot = jnp.concatenate([k1 * cosine - k2 * sine, k2 * cosine + k1 * sine], axis=-1).astype(BF16)
    own = jnp.stack([key_rot, values])[None]
    cosf = jnp.concatenate([cosine, cosine], axis=1)
    sinf = jnp.concatenate([-sine, sine], axis=1)

    near1 = from_y(cotangent, 1)
    near3 = from_y(cotangent, 3)
    far0 = swap(cotangent, "xh")
    near2 = from_y(cotangent, 2)
    near = [cotangent, near1, near2, near3]
    far = [far0]
    for d in (1, 2, 3):
        far.append(from_y(far0, d))
    behind1 = along_z(own, 1)
    behind2 = along_z(own, 2)
    mine = jnp.concatenate([behind2, behind1, own])
    across = swap(mine, "xl")
    partner1 = swap(mine, "c")
    partner2 = swap(across, "c")
    panels = (mine, across, partner1, partner2)

    w2 = jnp.transpose(out_weight, (1, 0, 2)).reshape(2 * HD, 4608)

    steps = jnp.arange(SLOTS, dtype=jnp.int32)
    panel, member = steps // 4, steps % 4
    rel = member ^ lane
    slot = (((rel & 1) << 1) | (rel >> 1)) * PANELS + panel
    index = steps - lane
    valid = (index >= 0) & (index < TILES) & (ctx - (TILES - 1) + index >= 0)
    flag = jnp.where(valid, jnp.where(index == 0, 1, jnp.where(index == TILES - 1, 2, 3)), 0)
    tile = jnp.clip(index, 0, TILES - 1)

    e, g, qr, attn, linv, kv, attn_t = forward(slot, tile, flag, queries, cosf, sinf, panels)

    shared = (w2, qr, attn, linv, cosf, sinf, kv, e, g)
    first = backward(slot, tile, flag, jnp.stack([y, xh]), near, *shared, None)
    keep, send, query_grad = backward(slot, tile, flag, jnp.stack([y, 1 - xh]), far, *shared, first)

    got = swap(send, "c")
    both = keep.astype(F32) + got.astype(F32)
    turned = [swap(both[PANELS + p].astype(BF16), "xl") for p in range(PANELS)]
    total = [both[p] + turned[p].astype(F32) for p in range(PANELS)]
    middle = total[1] + along_z(total[0].astype(BF16), -1).astype(F32)
    final = total[2] + along_z(middle.astype(BF16), -1).astype(F32)

    wkeep, wsend = weight(jnp.stack([y, xh, c]), near + far, attn_t)
    wgot = swap(wsend, "c")
    wsum = (wkeep + wgot.astype(F32)).reshape(2, 64, 4608)
    wgive = lax.dynamic_index_in_dim(wsum, 1 - xl, 0, False).astype(BF16)
    wown = lax.dynamic_index_in_dim(wsum, xl, 0, False)
    wback = swap(wgive, "xl")
    wz = (wown + wback.astype(F32)).astype(BF16).reshape(8, 8, 4608)
    wz = lax.all_to_all(wz, "z", 0, 0, tiled=True)
    weight_grad = jnp.sum(wz.astype(F32), axis=0).reshape(4, 2, 4608)

    gk = final[0]
    g1, g2 = gk[: HD // 2], gk[HD // 2 :]
    ct, st = cosine.T, sine.T
    key_grad = jnp.concatenate([g1 * ct + g2 * st, g2 * ct - g1 * st], axis=0).T
    value_grad = final[1].T
    return query_grad, key_grad, value_grad, weight_grad


def solution(mesh):
    fine = Mesh(mesh.devices.reshape(8, 2, 2, 2, 4), CTX + HEAD)
    placed = (P(CTX, HEAD), P(CTX, HEAD), P(CTX, HEAD), P(None, HEAD, None), P(CTX + HEAD, None))
    return jax.shard_map(
        local,
        mesh=fine,
        in_specs=placed,
        out_specs=(P(CTX, HEAD), P(CTX, HEAD), P(CTX, HEAD), P(CTX, HEAD, None)),
        check_vma=False,
    )
```

```python
import jax
import jax.numpy as jnp
import numpy as np
from jax import lax
from jax.experimental import pallas as pl
from jax.experimental.pallas import tpu as pltpu
from jax.sharding import Mesh, PartitionSpec as P

SOFT_CAP = 50.0
QUERY_MULTIPLIER = 144.0 ** (-0.5)
ROPE_BASE = 10000.0
LOG2E = 1.4426950408889634
CTX = ("z", "xl", "c")
HEAD = ("xh", "y")
TOK = 512
HALF = 256
HD = 128
PANELS = 3
SLOTS = 12
TILES = 9
NT = (((1,), (1,)), ((), ()))
F32 = jnp.float32
BF16 = jnp.bfloat16


def permute(x, axis, pairs):
    return lax.ppermute(x, axis, pairs)


def from_y(x, d):
    return permute(x, "y", [((i + d) % 4, i) for i in range(4)])


def swap(x, axis):
    return permute(x, axis, [(0, 1), (1, 0)])


def along_z(x, step):
    return permute(x, "z", [(i, i + step) for i in range(8) if 0 <= i + step < 8])


FREQUENCY = np.asarray([ROPE_BASE ** (-2.0 * (n % (HD // 2)) / HD) for n in range(HD)], np.float32)
SIGN = np.asarray([-1.0 if n < HD // 2 else 1.0 for n in range(HD)], np.float32)


def tables(first_row):
    positions = first_row + jnp.arange(TOK, dtype=jnp.int32)
    angles = positions.astype(F32)[:, None] * FREQUENCY[None, :]
    return jnp.cos(angles), SIGN[None, :] * jnp.sin(angles)


def place_of(info, i):
    rel = (i & 3) ^ info[0]
    return ((rel & 1) << 1) | (rel >> 1)


def tile_of(info, i):
    return jnp.clip(i - info[0], 0, TILES - 1)


def flag_of(info, i):
    index = i - info[0]
    valid = (index >= 0) & (index < TILES) & (info[1] - (TILES - 1) + index >= 0)
    return jnp.where(valid, jnp.where(index == 0, 1, jnp.where(index == TILES - 1, 2, 3)), 0)


def half_of(info, which):
    return info[3] if which == 1 else 1 - info[3]


def ndot(a, b):
    return jnp.dot(a, b, preferred_element_type=F32)


def tdot(a, b):
    return lax.dot_general(a, b, NT, preferred_element_type=F32)


def turn_kernel(k_ref, v_ref, cos_ref, sin_ref, own_ref):
    x = k_ref[...].astype(F32)
    own_ref[0, 0] = (x * cos_ref[...] + pltpu.roll(x, HD // 2, 1) * sin_ref[...]).astype(BF16)
    own_ref[0, 1] = v_ref[...]


def turn(keys, values, cosf, sinf):
    whole = lambda *shape: pl.BlockSpec(shape, lambda i, *_: (0,) * len(shape))
    return pl.pallas_call(
        turn_kernel,
        out_shape=jax.ShapeDtypeStruct((1, 2, TOK, HD), BF16),
        grid=(1,),
        in_specs=[whole(TOK, HD)] * 4,
        out_specs=whole(1, 2, TOK, HD),
        compiler_params=pltpu.CompilerParams(dimension_semantics=("arbitrary",), vmem_limit_bytes=60 << 20),
        cost_estimate=pl.CostEstimate(flops=500_000, bytes_accessed=1_000_000, transcendentals=0),
        name="turn",
    )(keys, values, cosf, sinf)


def load_pair(place, refs, pair):
    for n, ref in enumerate(refs):

        @pl.when(place == n)
        def _():
            pair[...] = ref[0]


def forward_kernel(
    info, q_ref, cos_ref, sin_ref, r0, r2, r1, r3, e_ref, g_ref, qr_ref, at_ref, li_ref, pt_ref, acc, pair
):
    step = pl.program_id(0)
    flag = flag_of(info, step)

    @pl.when(step == 0)
    def _():
        acc[...] = jnp.zeros_like(acc)
        cosine = cos_ref[...]
        sine = sin_ref[...]
        for h in range(2):
            x = q_ref[:, h * HD : (h + 1) * HD].astype(F32)
            qr_ref[:, h * HD : (h + 1) * HD] = (x * cosine + pltpu.roll(x, HD // 2, 1) * sine).astype(BF16)

    load_pair(place_of(info, step), (r0, r2, r1, r3), pair)

    def body(mode):
        key = pair[0]
        value = jnp.concatenate([pair[1], jnp.ones((TOK, HD), BF16)], axis=1)
        rows = HALF
        for h in range(2):
            for part in range(TOK // rows):
                at = pl.ds(part * rows, rows)
                s = tdot(qr_ref[at, h * HD : (h + 1) * HD], key)
                th = jnp.tanh(s * (QUERY_MULTIPLIER / SOFT_CAP))
                ex = jnp.exp2(th * (SOFT_CAP * LOG2E))
                if mode:
                    t = lax.broadcasted_iota(jnp.int32, (rows, TOK), 0) + part * rows
                    u = lax.broadcasted_iota(jnp.int32, (rows, TOK), 1)
                    ex = jnp.where(u > t if mode == 1 else u <= t, ex, 0.0)
                eb = ex.astype(BF16)
                e_ref[0, h, at, :] = eb
                g_ref[0, h, at, :] = (ex * (1.0 - th * th)).astype(BF16)
                acc[h, at, :] += ndot(eb, value)

    @pl.when(flag == 1)
    def _():
        body(1)

    @pl.when(flag == 2)
    def _():
        body(2)

    @pl.when(flag == 3)
    def _():
        body(0)

    @pl.when(step == SLOTS - 1)
    def _():
        for h in range(2):
            inverse = 1.0 / acc[h, :, HD:]
            at_ref[:, h * HD : (h + 1) * HD] = (acc[h, :, :HD] * inverse).astype(BF16)
            li_ref[:, h * HD : (h + 1) * HD] = inverse
        row = lax.broadcasted_iota(jnp.int32, (2 * HD, 2 * HD), 0)
        col = lax.broadcasted_iota(jnp.int32, (2 * HD, 2 * HD), 1)
        core, left, plane, four, head = row // 128, (row // 64) % 2, (row // 8) % 8, (row // 2) % 4, row % 2
        source = head * HD + plane * 16 + left * 8 + core * 4 + four
        pick = jnp.where(col == source, 1.0, 0.0).astype(BF16)
        pt_ref[...] = tdot(pick, at_ref[...]).astype(BF16)


def forward(info, queries, cosf, sinf, panels):
    whole = lambda *shape: pl.BlockSpec(shape, lambda i, *_: (0,) * len(shape))
    sds = jax.ShapeDtypeStruct
    eg = pl.BlockSpec((1, 2, TOK, TOK), lambda i, f: (tile_of(f, i), 0, 0, 0))
    return pl.pallas_call(
        forward_kernel,
        out_shape=(
            sds((TILES, 2, TOK, TOK), BF16),
            sds((TILES, 2, TOK, TOK), BF16),
            sds((TOK, 2 * HD), BF16),
            sds((TOK, 2 * HD), BF16),
            sds((TOK, 2 * HD), F32),
            sds((2 * HD, TOK), BF16),
        ),
        grid_spec=pltpu.PrefetchScalarGridSpec(
            num_scalar_prefetch=1,
            grid=(SLOTS,),
            in_specs=[
                whole(TOK, 2 * HD),
                whole(TOK, HD),
                whole(TOK, HD),
                *([pl.BlockSpec((1, 2, TOK, HD), lambda i, f: (i // 4, 0, 0, 0))] * 4),
            ],
            out_specs=(
                eg,
                eg,
                whole(TOK, 2 * HD),
                whole(TOK, 2 * HD),
                whole(TOK, 2 * HD),
                whole(2 * HD, TOK),
            ),
            scratch_shapes=[pltpu.VMEM((2, TOK, 2 * HD), F32), pltpu.VMEM((2, TOK, HD), BF16)],
        ),
        compiler_params=pltpu.CompilerParams(dimension_semantics=("arbitrary",), vmem_limit_bytes=60 << 20),
        cost_estimate=pl.CostEstimate(flops=10_000_000_000, bytes_accessed=24_000_000, transcendentals=10_000_000),
        name="attend",
    )(info, queries, cosf, sinf, *panels)


CARRY = (
    ((HALF, 2 * HD), BF16),
    ((2, HALF, HD), F32),
    ((2, HD, HALF), BF16),
    ((2, HD, HALF), BF16),
    ((2, HALF, HD), F32),
)


def backward_kernel(base, count, has_cots, has_prev, final, info, *refs):
    refs = list(refs)
    take = lambda n: [refs.pop(0) for _ in range(n)]
    cots = take(5) if has_cots else []
    carry_in = [] if has_cots else take(5)
    q_ref, at_ref, li_ref, cos_ref, sin_ref = take(5)
    pairs = take(4)
    e_ref, g_ref = take(2)
    if has_prev:
        (prev_ref,) = take(1)
        if final:
            take(1)
        keep_ref, send_ref = take(2)
    else:
        (part_ref,) = take(1)
    qg_ref = take(1)[0] if final else None
    carry_out = [] if final else take(5)
    cs, do, dl, qt, dt, dq, pair = refs
    work = (do, dl, qt, dt, dq)
    step = pl.program_id(0)
    flag = flag_of(info, base + step)

    @pl.when(step == 0)
    def _():
        if has_cots:
            y = info[2]
            for d, ref in enumerate(cots[:4]):
                row = pl.multiple_of(lax.rem(y + d, 4) * 64, 64)
                cs[pl.ds(row, 64), :] = ref[...]
            do[...] = tdot(cs[...], cots[4][...]).astype(BF16)
            for h in range(2):
                col = slice(h * HD, (h + 1) * HD)
                grad = do[:, col].astype(F32)
                inverse = li_ref[:, col]
                total = jnp.sum(grad * at_ref[:, col].astype(F32), axis=1, keepdims=True)
                dl[h] = jnp.broadcast_to(total, (HALF, HD))
                dt[h] = (grad * inverse).T.astype(BF16)
                qt[h] = (q_ref[:, col].astype(F32) * (inverse * QUERY_MULTIPLIER)).T.astype(BF16)
            dq[...] = jnp.zeros_like(dq)
        else:
            for a, b in zip(work, carry_in):
                a[...] = b[...]

    place = place_of(info, base + step)
    load_pair(place, pairs, pair)

    def put(dk, dv):
        if not has_prev:
            part_ref[0, 0] = dk
            part_ref[0, 1] = dv
            return

        @pl.when(place < 2)
        def _():
            keep_ref[place, 0] = dk
            keep_ref[place, 1] = dv

        @pl.when(place >= 2)
        def _():
            send_ref[place - 2, 0] = dk
            send_ref[place - 2, 1] = dv

    @pl.when(flag > 0)
    def _():
        key = pair[0]
        value = pair[1]
        dk = jnp.zeros((HD, TOK), F32)
        dv = jnp.zeros((HD, TOK), F32)
        for h in range(2):
            dp = tdot(do[:, h * HD : (h + 1) * HD], value)
            x = (g_ref[0, h].astype(F32) * (dp - dl[h][:, :1])).astype(BF16)
            dq[h] += ndot(x, key)
            dk += ndot(qt[h], x)
            dv += ndot(dt[h], e_ref[0, h])
        if has_prev:
            dk = dk + prev_ref[0, 0].astype(F32)
            dv = dv + prev_ref[0, 1].astype(F32)
        put(dk.astype(BF16), dv.astype(BF16))

    if has_prev:

        @pl.when(flag == 0)
        def _():
            zero = jnp.zeros((HD, TOK), BF16)
            put(zero, zero)

    @pl.when(step == count - 1)
    def _():
        if final:
            cosine = cos_ref[...]
            sine = sin_ref[...]
            for h in range(2):
                col = slice(h * HD, (h + 1) * HD)
                g = dq[h] * (li_ref[:, col] * QUERY_MULTIPLIER)
                qg_ref[:, col] = g * cosine - pltpu.roll(g, HD // 2, 1) * sine
        else:
            for a, b in zip(carry_out, work):
                a[...] = b[...]


def backward(base, count, which, info, rows, panels, e, g, cots=None, w2=None, carry=None, prev=None, grad=None):
    has_cots, has_prev = cots is not None, prev is not None
    final = base + count == SLOTS
    sds = jax.ShapeDtypeStruct
    whole = lambda *shape: pl.BlockSpec(shape, lambda i, *_: (0,) * len(shape))
    tok = lambda width: pl.BlockSpec((HALF, width), lambda i, f: (half_of(f, which), 0))
    eg = pl.BlockSpec((1, 2, HALF, TOK), lambda i, f: (tile_of(f, base + i), 0, half_of(f, which), 0))
    part = pl.BlockSpec((1, 2, HD, TOK), lambda i, f: ((base + i) // 4 * 4 + place_of(f, base + i), 0, 0, 0))
    ins, args, alias = [], [], {}
    if has_cots:
        ins += [whole(64, 4608)] * 4 + [whole(2 * HD, 4608)]
        args += [*cots, w2]
    else:
        ins += [whole(*shape) for shape, _ in CARRY]
        args += list(carry)
    ins += [tok(2 * HD), tok(2 * HD), tok(2 * HD), tok(HD), tok(HD)]
    args += list(rows)
    ins += [pl.BlockSpec((1, 2, TOK, HD), lambda i, f: ((base + i) // 4, 0, 0, 0))] * 4 + [eg, eg]
    args += [*panels, e, g]
    if has_prev:
        ins += [part]
        args += [prev]
        outs = [whole(2, 2, HD, TOK)] * 2
        shapes = [sds((2, 2, HD, TOK), BF16)] * 2
    else:
        outs = [part]
        shapes = [sds((SLOTS, 2, HD, TOK), BF16)]
    if final:
        if grad is not None:
            ins += [pl.BlockSpec(memory_space=pl.ANY)]
            args += [grad]
            alias = {len(args): len(outs)}
        outs += [tok(2 * HD)]
        shapes += [sds((TOK, 2 * HD), F32)]
    else:
        outs += [whole(*shape) for shape, _ in CARRY]
        shapes += [sds(*c) for c in CARRY]

    def kernel(*refs):
        backward_kernel(base, count, has_cots, has_prev, final, *refs)

    return pl.pallas_call(
        kernel,
        out_shape=shapes,
        grid_spec=pltpu.PrefetchScalarGridSpec(
            num_scalar_prefetch=1,
            grid=(count,),
            in_specs=ins,
            out_specs=outs,
            scratch_shapes=[
                pltpu.VMEM((HALF, 4608) if has_cots else (16, 128), BF16),
                *(pltpu.VMEM(*c) for c in CARRY),
                pltpu.VMEM((2, TOK, HD), BF16),
            ],
        ),
        compiler_params=pltpu.CompilerParams(dimension_semantics=("arbitrary",), vmem_limit_bytes=60 << 20),
        input_output_aliases=alias,
        cost_estimate=pl.CostEstimate(flops=700_000_000 * count, bytes_accessed=2_000_000 * count, transcendentals=0),
    )(info, *args)


def weight_kernel(where, *refs):
    cots = refs[:8]
    at_ref, keep_ref, send_ref, cs = refs[8:]
    y, own, core = where[2], where[3], where[4]
    for n, ref in enumerate(cots):
        base = own if n < 4 else 1 - own
        row = pl.multiple_of(base * HALF + lax.rem(y + n % 4, 4) * 64, 64)
        cs[pl.ds(row, 64), :] = ref[...]
    rows = cs[...]
    mine = pl.multiple_of(core * HD, HD)
    other = pl.multiple_of((1 - core) * HD, HD)
    keep_ref[...] = ndot(at_ref[pl.ds(mine, HD), :], rows)
    send_ref[...] = ndot(at_ref[pl.ds(other, HD), :], rows).astype(BF16)


def weight(where, cots, attn_t):
    chunk = 1152
    sds = jax.ShapeDtypeStruct
    block = lambda rows: pl.BlockSpec((rows, chunk), lambda i, w: (0, i))
    return pl.pallas_call(
        weight_kernel,
        out_shape=(sds((HD, 4608), F32), sds((HD, 4608), BF16)),
        grid_spec=pltpu.PrefetchScalarGridSpec(
            num_scalar_prefetch=1,
            grid=(4608 // chunk,),
            in_specs=[block(64)] * 8 + [pl.BlockSpec((2 * HD, TOK), lambda i, w: (0, 0))],
            out_specs=(block(HD), block(HD)),
            scratch_shapes=[pltpu.VMEM((TOK, chunk), BF16)],
        ),
        compiler_params=pltpu.CompilerParams(dimension_semantics=("arbitrary",), vmem_limit_bytes=60 << 20),
        cost_estimate=pl.CostEstimate(flops=1_300_000_000, bytes_accessed=9_000_000, transcendentals=0),
        name="weigh",
    )(where, *cots, attn_t)


def settle_kernel(own_ref, left_ref, down_ref, cos_ref, sin_ref, kg_ref, vg_ref):
    both = own_ref[0] + left_ref[...].astype(F32) + down_ref[...].astype(F32)
    g = both[0].T
    kg_ref[...] = g * cos_ref[...] - pltpu.roll(g, HD // 2, 1) * sin_ref[...]
    vg_ref[...] = both[1].T


def settle(both, left, down, cosf, sinf):
    whole = lambda *shape: pl.BlockSpec(shape, lambda i, *_: (0,) * len(shape))
    sds = jax.ShapeDtypeStruct
    return pl.pallas_call(
        settle_kernel,
        out_shape=(sds((TOK, HD), F32), sds((TOK, HD), F32)),
        grid=(1,),
        in_specs=[whole(1, 2, HD, TOK), whole(2, HD, TOK), whole(2, HD, TOK), whole(TOK, HD), whole(TOK, HD)],
        out_specs=(whole(TOK, HD), whole(TOK, HD)),
        compiler_params=pltpu.CompilerParams(dimension_semantics=("arbitrary",), vmem_limit_bytes=60 << 20),
        cost_estimate=pl.CostEstimate(flops=500_000, bytes_accessed=2_000_000, transcendentals=0),
        name="settle",
    )(both, left, down, cosf, sinf)


def local(queries, keys, values, out_weight, cotangent):
    z, xl, c = (lax.axis_index(a) for a in CTX)
    xh, y = (lax.axis_index(a) for a in HEAD)
    lane = xl * 2 + c
    ctx = z * 4 + lane
    cosf, sinf = tables(ctx * TOK)

    info = jnp.stack([lane, ctx, y, xh, c]).astype(jnp.int32)

    own = turn(keys, values, cosf, sinf)
    behind1 = along_z(own, 1)
    behind2 = along_z(own, 2)
    across0 = swap(own, "xl")
    near1 = from_y(cotangent, 1)
    near3 = from_y(cotangent, 3)
    far0 = swap(cotangent, "xh")
    near2 = from_y(cotangent, 2)
    near = [cotangent, near1, near2, near3]
    far = [far0]
    for d in (1, 2, 3):
        far.append(from_y(far0, d))
    back = jnp.concatenate([behind2, behind1])
    across = swap(back, "xl")
    mine = jnp.concatenate([back, own])
    partner1 = swap(mine, "c")
    across = jnp.concatenate([across, across0])
    partner2 = swap(across, "c")
    panels = (mine, across, partner1, partner2)

    w2 = jnp.transpose(out_weight, (1, 0, 2)).reshape(2 * HD, 4608)

    e, g, qr, attn, linv, attn_t = forward(info, queries, cosf, sinf, panels)
    rows = (qr, attn, linv, cosf, sinf)
    prev, half = backward(0, SLOTS, 1, info, rows, panels, e, g, cots=near, w2=w2)

    wkeep, wsend = weight(info, near + far, attn_t)
    wgot = swap(wsend, "c")
    wsum = (wkeep + wgot.astype(F32)).reshape(2, 64, 4608)
    wgive = lax.dynamic_index_in_dim(wsum, 1 - xl, 0, False).astype(BF16)
    wown = lax.dynamic_index_in_dim(wsum, xl, 0, False)
    wback = swap(wgive, "xl")
    wz = (wown + wback.astype(F32)).astype(BF16).reshape(8, 8, 4608)
    wz = lax.all_to_all(wz, "z", 0, 0, tiled=True)
    weight_grad = jnp.sum(wz.astype(F32), axis=0).reshape(4, 2, 4608)

    total = []
    carry = None
    for p in range(PANELS):
        out = backward(
            p * 4, 4, 2, info, rows, panels, e, g,
            cots=far if p == 0 else None, w2=w2 if p == 0 else None, carry=carry, prev=prev,
            grad=half if p == PANELS - 1 else None,
        )
        keep, send, *carry = out
        got = swap(send, "c")
        both = keep.astype(F32) + got.astype(F32)
        give = both[1].astype(BF16)
        turned = swap(give, "xl")
        total.append((both, turned))
    (query_grad,) = carry
    down1 = along_z((total[0][0][0] + total[0][1].astype(F32)).astype(BF16), -1)
    down0 = along_z((total[1][0][0] + total[1][1].astype(F32) + down1.astype(F32)).astype(BF16), -1)
    key_grad, value_grad = settle(*total[2], down0, cosf, sinf)
    return query_grad, key_grad, value_grad, weight_grad


def solution(mesh):
    fine = Mesh(mesh.devices.reshape(8, 2, 2, 2, 4), CTX + HEAD)
    placed = (P(CTX, HEAD), P(CTX, HEAD), P(CTX, HEAD), P(None, HEAD, None), P(CTX + HEAD, None))
    return jax.shard_map(
        local,
        mesh=fine,
        in_specs=placed,
        out_specs=(P(CTX, HEAD), P(CTX, HEAD), P(CTX, HEAD), P(CTX, HEAD, None)),
        check_vma=False,
    )
```

```python
import jax
import jax.numpy as jnp
import numpy as np
from jax import lax
from jax.experimental import pallas as pl
from jax.experimental.pallas import tpu as pltpu
from jax.sharding import Mesh, PartitionSpec as P

SOFT_CAP = 50.0
QUERY_MULTIPLIER = 144.0 ** (-0.5)
ROPE_BASE = 10000.0
LOG2E = 1.4426950408889634
CTX = ("z", "xl", "c")
HEAD = ("xh", "y")
TOK = 512
HALF = 256
HD = 128
PANELS = 3
SLOTS = 12
TILES = 9
PACK = 2
NT = (((1,), (1,)), ((), ()))
F32 = jnp.float32
BF16 = jnp.bfloat16


def permute(x, axis, pairs):
    return lax.ppermute(x, axis, pairs)


def from_y(x, d):
    return permute(x, "y", [((i + d) % 4, i) for i in range(4)])


def swap(x, axis):
    return permute(x, axis, [(0, 1), (1, 0)])


def along_z(x, step):
    return permute(x, "z", [(i, i + step) for i in range(8) if 0 <= i + step < 8])


FREQUENCY = np.asarray([ROPE_BASE ** (-2.0 * (n % (HD // 2)) / HD) for n in range(HD)], np.float32)
SIGN = np.asarray([-1.0 if n < HD // 2 else 1.0 for n in range(HD)], np.float32)


def tables(first_row):
    positions = first_row + jnp.arange(TOK, dtype=jnp.int32)
    angles = positions.astype(F32)[:, None] * FREQUENCY[None, :]
    return jnp.cos(angles), SIGN[None, :] * jnp.sin(angles)


def place_of(info, i):
    rel = (i & 3) ^ info[0]
    return ((rel & 1) << 1) | (rel >> 1)


def flag_of(info, i):
    index = i - info[0]
    valid = (index >= 0) & (index < TILES) & (info[1] - (TILES - 1) + index >= 0)
    return jnp.where(valid, jnp.where(index == 0, 1, jnp.where(index == TILES - 1, 2, 3)), 0)


def half_of(info, which):
    return info[3] if which == 1 else 1 - info[3]


def ndot(a, b):
    return jnp.dot(a, b, preferred_element_type=F32)


def tdot(a, b):
    return lax.dot_general(a, b, NT, preferred_element_type=F32)


def turn_kernel(k_ref, v_ref, cos_ref, sin_ref, own_ref):
    x = k_ref[...].astype(F32)
    own_ref[0, 0] = (x * cos_ref[...] + pltpu.roll(x, HD // 2, 1) * sin_ref[...]).astype(BF16)
    own_ref[0, 1] = v_ref[...]


def turn(keys, values, cosf, sinf):
    whole = lambda *shape: pl.BlockSpec(shape, lambda i, *_: (0,) * len(shape))
    return pl.pallas_call(
        turn_kernel,
        out_shape=jax.ShapeDtypeStruct((1, 2, TOK, HD), BF16),
        grid=(1,),
        in_specs=[whole(TOK, HD)] * 4,
        out_specs=whole(1, 2, TOK, HD),
        compiler_params=pltpu.CompilerParams(dimension_semantics=("arbitrary",), vmem_limit_bytes=46 << 20),
        cost_estimate=pl.CostEstimate(flops=500_000, bytes_accessed=1_000_000, transcendentals=0),
        name="turn",
    )(keys, values, cosf, sinf)


def load_pair(place, refs, pair):
    for n, ref in enumerate(refs):

        @pl.when(place == n)
        def _():
            pair[...] = ref[0]


def forward_kernel(
    info, q_ref, cos_ref, sin_ref, r0, r2, r1, r3, eg_ref, qr_ref, at_ref, li_ref, pt_ref, acc, pair
):
    step = pl.program_id(0)

    @pl.when(step == 0)
    def _():
        acc[...] = jnp.zeros_like(acc)
        cosine = cos_ref[...]
        sine = sin_ref[...]
        for h in range(2):
            x = q_ref[:, h * HD : (h + 1) * HD].astype(F32)
            qr_ref[:, h * HD : (h + 1) * HD] = (x * cosine + pltpu.roll(x, HD // 2, 1) * sine).astype(BF16)

    def one(u, _):
        slot = step * PACK + u
        flag = flag_of(info, slot)

        @pl.when(flag > 0)
        def _():
            load_pair(place_of(info, slot), (r0, r2, r1, r3), pair)

        def body(mode):
            key = pair[0]
            value = jnp.concatenate([pair[1], jnp.ones((TOK, HD), BF16)], axis=1)
            rows = HALF
            for h in range(2):
                for part in range(TOK // rows):
                    at = pl.ds(part * rows, rows)
                    s = tdot(qr_ref[at, h * HD : (h + 1) * HD], key)
                    th = jnp.tanh(s * (QUERY_MULTIPLIER / SOFT_CAP))
                    ex = jnp.exp2(th * (SOFT_CAP * LOG2E))
                    if mode:
                        t = lax.broadcasted_iota(jnp.int32, (rows, TOK), 0) + part * rows
                        k = lax.broadcasted_iota(jnp.int32, (rows, TOK), 1)
                        ex = jnp.where(k > t if mode == 1 else k <= t, ex, 0.0)
                    eb = ex.astype(BF16)
                    eg_ref[u, 0, h, at, :] = eb
                    eg_ref[u, 1, h, at, :] = (ex * (1.0 - th * th)).astype(BF16)
                    acc[h, at, :] += ndot(eb, value)

        for want, mode in ((1, 1), (2, 2), (3, 0)):

            @pl.when(flag == want)
            def _():
                body(mode)

        return 0

    lax.fori_loop(0, PACK, one, 0)

    @pl.when(step == SLOTS // PACK - 1)
    def _():
        for h in range(2):
            inverse = 1.0 / acc[h, :, HD:]
            at_ref[:, h * HD : (h + 1) * HD] = (acc[h, :, :HD] * inverse).astype(BF16)
            li_ref[:, h * HD : (h + 1) * HD] = inverse
        row = lax.broadcasted_iota(jnp.int32, (2 * HD, 2 * HD), 0)
        col = lax.broadcasted_iota(jnp.int32, (2 * HD, 2 * HD), 1)
        core, left, plane, four, head = row // 128, (row // 64) % 2, (row // 8) % 8, (row // 2) % 4, row % 2
        source = head * HD + plane * 16 + left * 8 + core * 4 + four
        pick = jnp.where(col == source, 1.0, 0.0).astype(BF16)
        pt_ref[...] = tdot(pick, at_ref[...]).astype(BF16)


def forward(info, queries, cosf, sinf, panels):
    whole = lambda *shape: pl.BlockSpec(shape, lambda i, *_: (0,) * len(shape))
    sds = jax.ShapeDtypeStruct
    eg = pl.BlockSpec((PACK, 2, 2, TOK, TOK), lambda i, f: (i, 0, 0, 0, 0))
    return pl.pallas_call(
        forward_kernel,
        out_shape=(
            sds((SLOTS, 2, 2, TOK, TOK), BF16),
            sds((TOK, 2 * HD), BF16),
            sds((TOK, 2 * HD), BF16),
            sds((TOK, 2 * HD), F32),
            sds((2 * HD, TOK), BF16),
        ),
        grid_spec=pltpu.PrefetchScalarGridSpec(
            num_scalar_prefetch=1,
            grid=(SLOTS // PACK,),
            in_specs=[
                whole(TOK, 2 * HD),
                whole(TOK, HD),
                whole(TOK, HD),
                *([pl.BlockSpec((1, 2, TOK, HD), lambda i, f: (i // (4 // PACK), 0, 0, 0))] * 4),
            ],
            out_specs=(
                eg,
                whole(TOK, 2 * HD),
                whole(TOK, 2 * HD),
                whole(TOK, 2 * HD),
                whole(2 * HD, TOK),
            ),
            scratch_shapes=[pltpu.VMEM((2, TOK, 2 * HD), F32), pltpu.VMEM((2, TOK, HD), BF16)],
        ),
        compiler_params=pltpu.CompilerParams(dimension_semantics=("arbitrary",), vmem_limit_bytes=46 << 20),
        cost_estimate=pl.CostEstimate(flops=10_000_000_000, bytes_accessed=24_000_000, transcendentals=10_000_000),
        name="attend",
    )(info, queries, cosf, sinf, *panels)


CARRY = (
    ((HALF, 2 * HD), BF16),
    ((2, HALF, HD), F32),
    ((2, HD, HALF), BF16),
    ((2, HD, HALF), BF16),
    ((2, HALF, HD), F32),
)


def backward_kernel(base, count, has_cots, has_prev, final, info, *refs):
    refs = list(refs)
    take = lambda n: [refs.pop(0) for _ in range(n)]
    cots = take(5) if has_cots else []
    carry_in = [] if has_cots else take(5)
    q_ref, at_ref = take(2) if has_cots else (None, None)
    li_ref = take(1)[0] if has_cots or final else None
    cos_ref, sin_ref = take(2) if final else (None, None)
    pairs = take(4)
    (eg_ref,) = take(1)
    if has_prev:
        (prev_ref,) = take(1)
        if final:
            take(1)
        keep_ref, send_ref = take(2)
    else:
        (part_ref,) = take(1)
    qg_ref = take(1)[0] if final else None
    carry_out = [] if final else take(5 if has_cots else 1)
    cs, do, dl, qt, dt, dq, pair = refs
    work = (do, dl, qt, dt, dq)
    if not has_cots:
        do, dl, qt, dt = carry_in[:4]
    step = pl.program_id(0)

    @pl.when(step == 0)
    def _():
        if has_cots:
            y = info[2]
            for d, ref in enumerate(cots[:4]):
                row = pl.multiple_of(lax.rem(y + d, 4) * 64, 64)
                cs[pl.ds(row, 64), :] = ref[...]
            do[...] = tdot(cs[...], cots[4][...]).astype(BF16)
            for h in range(2):
                col = slice(h * HD, (h + 1) * HD)
                grad = do[:, col].astype(F32)
                inverse = li_ref[:, col]
                total = jnp.sum(grad * at_ref[:, col].astype(F32), axis=1, keepdims=True)
                dl[h] = jnp.broadcast_to(total, (HALF, HD))
                dt[h] = (grad * inverse).T.astype(BF16)
                qt[h] = (q_ref[:, col].astype(F32) * (inverse * QUERY_MULTIPLIER)).T.astype(BF16)
            dq[...] = jnp.zeros_like(dq)
        else:
            dq[...] = carry_in[4][...]

    def one(u, _):
        slot = base + step * PACK + u
        place = place_of(info, slot)
        flag = flag_of(info, slot)

        def put(dk, dv):
            if not has_prev:
                part_ref[u, 0] = dk
                part_ref[u, 1] = dv
                return

            @pl.when(place < 2)
            def _():
                keep_ref[place, 0] = dk
                keep_ref[place, 1] = dv

            @pl.when(place >= 2)
            def _():
                send_ref[place - 2, 0] = dk
                send_ref[place - 2, 1] = dv

        @pl.when(flag > 0)
        def _():
            load_pair(place, pairs, pair)
            key = pair[0]
            value = pair[1]
            dk = jnp.zeros((HD, TOK), F32)
            dv = jnp.zeros((HD, TOK), F32)
            for h in range(2):
                dp = tdot(do[:, h * HD : (h + 1) * HD], value)
                x = (eg_ref[u, 1, h].astype(F32) * (dp - dl[h][:, :1])).astype(BF16)
                dq[h] += ndot(x, key)
                dk += ndot(qt[h], x)
                dv += ndot(dt[h], eg_ref[u, 0, h])
            if has_prev:
                dk = dk + prev_ref[u, 0].astype(F32)
                dv = dv + prev_ref[u, 1].astype(F32)
            put(dk.astype(BF16), dv.astype(BF16))

        if has_prev:

            @pl.when(flag == 0)
            def _():
                zero = jnp.zeros((HD, TOK), BF16)
                put(zero, zero)

        return 0

    lax.fori_loop(0, PACK, one, 0)

    @pl.when(step == count // PACK - 1)
    def _():
        if final:
            cosine = cos_ref[...]
            sine = sin_ref[...]
            for h in range(2):
                col = slice(h * HD, (h + 1) * HD)
                g = dq[h] * (li_ref[:, col] * QUERY_MULTIPLIER)
                qg_ref[:, col] = g * cosine - pltpu.roll(g, HD // 2, 1) * sine
        else:
            for a, b in zip(carry_out, work if has_cots else work[4:]):
                a[...] = b[...]


def backward(base, count, which, info, rows, panels, eg_all, cots=None, w2=None, carry=None, prev=None, grad=None):
    has_cots, has_prev = cots is not None, prev is not None
    final = base + count == SLOTS
    sds = jax.ShapeDtypeStruct
    whole = lambda *shape: pl.BlockSpec(shape, lambda i, *_: (0,) * len(shape))
    tok = lambda width: pl.BlockSpec((HALF, width), lambda i, f: (half_of(f, which), 0))
    eg = pl.BlockSpec((PACK, 2, 2, HALF, TOK), lambda i, f: (base // PACK + i, 0, 0, half_of(f, which), 0))
    part = pl.BlockSpec((PACK, 2, HD, TOK), lambda i, f: (base // PACK + i, 0, 0, 0))
    ins, args, alias = [], [], {}
    if has_cots:
        ins += [whole(64, 4608)] * 4 + [whole(2 * HD, 4608)]
        args += [*cots, w2]
    else:
        ins += [whole(*shape) for shape, _ in CARRY]
        args += list(carry)
    wanted = [has_cots, has_cots, has_cots or final, final, final]
    widths = [2 * HD, 2 * HD, 2 * HD, HD, HD]
    ins += [tok(n) for n, use in zip(widths, wanted) if use]
    args += [a for a, use in zip(rows, wanted) if use]
    ins += [pl.BlockSpec((1, 2, TOK, HD), lambda i, f: (base // 4 + i // (4 // PACK), 0, 0, 0))] * 4 + [eg]
    args += [*panels, eg_all]
    if has_prev:
        ins += [part]
        args += [prev]
        outs = [whole(2, 2, HD, TOK)] * 2
        shapes = [sds((2, 2, HD, TOK), BF16)] * 2
    else:
        outs = [part]
        shapes = [sds((SLOTS, 2, HD, TOK), BF16)]
    if final:
        if grad is not None:
            ins += [pl.BlockSpec(memory_space=pl.ANY)]
            args += [grad]
            alias = {len(args): len(outs)}
        outs += [tok(2 * HD)]
        shapes += [sds((TOK, 2 * HD), F32)]
    else:
        left = CARRY if has_cots else CARRY[4:]
        outs += [whole(*shape) for shape, _ in left]
        shapes += [sds(*c) for c in left]

    def kernel(*refs):
        backward_kernel(base, count, has_cots, has_prev, final, *refs)

    return pl.pallas_call(
        kernel,
        out_shape=shapes,
        grid_spec=pltpu.PrefetchScalarGridSpec(
            num_scalar_prefetch=1,
            grid=(count // PACK,),
            in_specs=ins,
            out_specs=outs,
            scratch_shapes=[
                pltpu.VMEM((HALF, 4608) if has_cots else (16, 128), BF16),
                *(pltpu.VMEM(*c) for c in CARRY),
                pltpu.VMEM((2, TOK, HD), BF16),
            ],
        ),
        compiler_params=pltpu.CompilerParams(dimension_semantics=("arbitrary",), vmem_limit_bytes=(60 if has_prev else 46) << 20),
        input_output_aliases=alias,
        cost_estimate=pl.CostEstimate(flops=700_000_000 * count, bytes_accessed=2_000_000 * count, transcendentals=0),
    )(info, *args)


def weight_kernel(where, *refs):
    cots = refs[:8]
    at_ref, keep_ref, send_ref, cs = refs[8:]
    y, own, core = where[2], where[3], where[4]
    for n, ref in enumerate(cots):
        base = own if n < 4 else 1 - own
        row = pl.multiple_of(base * HALF + lax.rem(y + n % 4, 4) * 64, 64)
        cs[pl.ds(row, 64), :] = ref[...]
    rows = cs[...]
    mine = pl.multiple_of(core * HD, HD)
    other = pl.multiple_of((1 - core) * HD, HD)
    keep_ref[...] = ndot(at_ref[pl.ds(mine, HD), :], rows)
    send_ref[...] = ndot(at_ref[pl.ds(other, HD), :], rows).astype(BF16)


def weight(where, cots, attn_t):
    chunk = 1152
    sds = jax.ShapeDtypeStruct
    block = lambda rows: pl.BlockSpec((rows, chunk), lambda i, w: (0, i))
    return pl.pallas_call(
        weight_kernel,
        out_shape=(sds((HD, 4608), F32), sds((HD, 4608), BF16)),
        grid_spec=pltpu.PrefetchScalarGridSpec(
            num_scalar_prefetch=1,
            grid=(4608 // chunk,),
            in_specs=[block(64)] * 8 + [pl.BlockSpec((2 * HD, TOK), lambda i, w: (0, 0))],
            out_specs=(block(HD), block(HD)),
            scratch_shapes=[pltpu.VMEM((TOK, chunk), BF16)],
        ),
        compiler_params=pltpu.CompilerParams(dimension_semantics=("arbitrary",), vmem_limit_bytes=46 << 20),
        cost_estimate=pl.CostEstimate(flops=1_300_000_000, bytes_accessed=9_000_000, transcendentals=0),
        name="weigh",
    )(where, *cots, attn_t)


def settle_kernel(own_ref, left_ref, down_ref, cos_ref, sin_ref, kg_ref, vg_ref):
    both = own_ref[0] + left_ref[...].astype(F32) + down_ref[...].astype(F32)
    g = both[0].T
    kg_ref[...] = g * cos_ref[...] - pltpu.roll(g, HD // 2, 1) * sin_ref[...]
    vg_ref[...] = both[1].T


def settle(both, left, down, cosf, sinf):
    whole = lambda *shape: pl.BlockSpec(shape, lambda i, *_: (0,) * len(shape))
    sds = jax.ShapeDtypeStruct
    return pl.pallas_call(
        settle_kernel,
        out_shape=(sds((TOK, HD), F32), sds((TOK, HD), F32)),
        grid=(1,),
        in_specs=[whole(1, 2, HD, TOK), whole(2, HD, TOK), whole(2, HD, TOK), whole(TOK, HD), whole(TOK, HD)],
        out_specs=(whole(TOK, HD), whole(TOK, HD)),
        compiler_params=pltpu.CompilerParams(dimension_semantics=("arbitrary",), vmem_limit_bytes=46 << 20),
        cost_estimate=pl.CostEstimate(flops=500_000, bytes_accessed=2_000_000, transcendentals=0),
        name="settle",
    )(both, left, down, cosf, sinf)


def local(queries, keys, values, out_weight, cotangent):
    z, xl, c = (lax.axis_index(a) for a in CTX)
    xh, y = (lax.axis_index(a) for a in HEAD)
    lane = xl * 2 + c
    ctx = z * 4 + lane
    cosf, sinf = tables(ctx * TOK)

    info = jnp.stack([lane, ctx, y, xh, c]).astype(jnp.int32)

    own = turn(keys, values, cosf, sinf)
    behind1 = along_z(own, 1)
    behind2 = along_z(own, 2)
    across0 = swap(own, "xl")
    near1 = from_y(cotangent, 1)
    near3 = from_y(cotangent, 3)
    far0 = swap(cotangent, "xh")
    near2 = from_y(cotangent, 2)
    near = [cotangent, near1, near2, near3]
    far = [far0]
    for d in (1, 2, 3):
        far.append(from_y(far0, d))
    back = jnp.concatenate([behind2, behind1])
    across = swap(back, "xl")
    mine = jnp.concatenate([back, own])
    partner1 = swap(mine, "c")
    across = jnp.concatenate([across, across0])
    partner2 = swap(across, "c")
    panels = (mine, across, partner1, partner2)

    w2 = jnp.transpose(out_weight, (1, 0, 2)).reshape(2 * HD, 4608)

    eg, qr, attn, linv, attn_t = forward(info, queries, cosf, sinf, panels)
    rows = (qr, attn, linv, cosf, sinf)
    prev, half = backward(0, SLOTS, 1, info, rows, panels, eg, cots=near, w2=w2)

    wkeep, wsend = weight(info, near + far, attn_t)
    wgot = swap(wsend, "c")
    wsum = (wkeep + wgot.astype(F32)).reshape(2, 64, 4608)
    wgive = lax.dynamic_index_in_dim(wsum, 1 - xl, 0, False).astype(BF16)
    wown = lax.dynamic_index_in_dim(wsum, xl, 0, False)
    wback = swap(wgive, "xl")
    wz = (wown + wback.astype(F32)).astype(BF16).reshape(8, 8, 4608)
    wz = lax.all_to_all(wz, "z", 0, 0, tiled=True)
    weight_grad = jnp.sum(wz.astype(F32), axis=0).reshape(4, 2, 4608)

    total = []
    carry = None
    for p in range(PANELS):
        out = backward(
            p * 4, 4, 2, info, rows, panels, eg,
            cots=far if p == 0 else None, w2=w2 if p == 0 else None, carry=carry, prev=prev,
            grad=half if p == PANELS - 1 else None,
        )
        keep, send, *after = out
        carry = after if len(after) != 1 or p == PANELS - 1 else [*carry[:4], *after]
        got = swap(send, "c")
        both = keep.astype(F32) + got.astype(F32)
        give = both[1].astype(BF16)
        turned = swap(give, "xl")
        total.append((both, turned))
    (query_grad,) = carry
    down1 = along_z((total[0][0][0] + total[0][1].astype(F32)).astype(BF16), -1)
    down0 = along_z((total[1][0][0] + total[1][1].astype(F32) + down1.astype(F32)).astype(BF16), -1)
    key_grad, value_grad = settle(*total[2], down0, cosf, sinf)
    return query_grad, key_grad, value_grad, weight_grad


def solution(mesh):
    fine = Mesh(mesh.devices.reshape(8, 2, 2, 2, 4), CTX + HEAD)
    placed = (P(CTX, HEAD), P(CTX, HEAD), P(CTX, HEAD), P(None, HEAD, None), P(CTX + HEAD, None))
    return jax.shard_map(
        local,
        mesh=fine,
        in_specs=placed,
        out_specs=(P(CTX, HEAD), P(CTX, HEAD), P(CTX, HEAD), P(CTX, HEAD, None)),
        check_vma=False,
    )
```

```python
import jax
import jax.numpy as jnp
import numpy as np
from jax import lax
from jax.experimental import pallas as pl
from jax.experimental.pallas import tpu as pltpu
from jax.sharding import Mesh, PartitionSpec as P

SOFT_CAP = 50.0
QUERY_MULTIPLIER = 144.0 ** (-0.5)
ROPE_BASE = 10000.0
LOG2E = 1.4426950408889634
CTX = ("z", "xl", "c")
HEAD = ("xh", "y")
TOK = 512
HALF = 256
HD = 128
PANELS = 3
SLOTS = 12
TILES = 9
PACK = 2
NT = (((1,), (1,)), ((), ()))
F32 = jnp.float32
BF16 = jnp.bfloat16


def permute(x, axis, pairs):
    return lax.ppermute(x, axis, pairs)


def from_y(x, d):
    return permute(x, "y", [((i + d) % 4, i) for i in range(4)])


def swap(x, axis):
    return permute(x, axis, [(0, 1), (1, 0)])


def along_z(x, step):
    return permute(x, "z", [(i, i + step) for i in range(8) if 0 <= i + step < 8])


FREQUENCY = np.asarray([ROPE_BASE ** (-2.0 * (n % (HD // 2)) / HD) for n in range(HD)], np.float32)
SIGN = np.asarray([-1.0 if n < HD // 2 else 1.0 for n in range(HD)], np.float32)


def tables(first_row):
    positions = first_row + jnp.arange(TOK, dtype=jnp.int32)
    angles = positions.astype(F32)[:, None] * FREQUENCY[None, :]
    return jnp.cos(angles), SIGN[None, :] * jnp.sin(angles)


def place_of(info, i):
    rel = (i & 3) ^ info[0]
    return ((rel & 1) << 1) | (rel >> 1)


def flag_of(info, i):
    index = i - info[0]
    valid = (index >= 0) & (index < TILES) & (info[1] - (TILES - 1) + index >= 0)
    return jnp.where(valid, jnp.where(index == 0, 1, jnp.where(index == TILES - 1, 2, 3)), 0)


def half_of(info, which):
    return info[3] if which == 1 else 1 - info[3]


def ndot(a, b):
    return jnp.dot(a, b, preferred_element_type=F32)


def tdot(a, b):
    return lax.dot_general(a, b, NT, preferred_element_type=F32)


def turn_kernel(k_ref, v_ref, cos_ref, sin_ref, own_ref):
    x = k_ref[...].astype(F32)
    own_ref[0, 0] = (x * cos_ref[...] + pltpu.roll(x, HD // 2, 1) * sin_ref[...]).astype(BF16)
    own_ref[0, 1] = v_ref[...]


def turn(keys, values, cosf, sinf):
    whole = lambda *shape: pl.BlockSpec(shape, lambda i, *_: (0,) * len(shape))
    return pl.pallas_call(
        turn_kernel,
        out_shape=jax.ShapeDtypeStruct((1, 2, TOK, HD), BF16),
        grid=(1,),
        in_specs=[whole(TOK, HD)] * 4,
        out_specs=whole(1, 2, TOK, HD),
        compiler_params=pltpu.CompilerParams(dimension_semantics=("arbitrary",), vmem_limit_bytes=46 << 20),
        cost_estimate=pl.CostEstimate(flops=500_000, bytes_accessed=1_000_000, transcendentals=0),
        name="turn",
    )(keys, values, cosf, sinf)


def load_pair(place, refs, pair):
    for n, ref in enumerate(refs):

        @pl.when(place == n)
        def _():
            pair[...] = ref[0]


def forward_kernel(
    info, q_ref, cos_ref, sin_ref, r0, r2, r1, r3, eg_ref, qr_ref, at_ref, li_ref, pt_ref, acc, pair
):
    step = pl.program_id(0)

    @pl.when(step == 0)
    def _():
        acc[...] = jnp.zeros_like(acc)
        cosine = cos_ref[...]
        sine = sin_ref[...]
        for h in range(2):
            x = q_ref[:, h * HD : (h + 1) * HD].astype(F32)
            qr_ref[:, h * HD : (h + 1) * HD] = (x * cosine + pltpu.roll(x, HD // 2, 1) * sine).astype(BF16)

    def one(u, _):
        slot = step * PACK + u
        flag = flag_of(info, slot)

        @pl.when(flag > 0)
        def _():
            load_pair(place_of(info, slot), (r0, r2, r1, r3), pair)

        def body(mode):
            key = pair[0]
            value = jnp.concatenate([pair[1], jnp.ones((TOK, HD), BF16)], axis=1)
            rows = HALF
            for h in range(2):
                for part in range(TOK // rows):
                    at = pl.ds(part * rows, rows)
                    s = tdot(qr_ref[at, h * HD : (h + 1) * HD], key)
                    th = jnp.tanh(s * (QUERY_MULTIPLIER / SOFT_CAP))
                    ex = jnp.exp2(th * (SOFT_CAP * LOG2E))
                    if mode:
                        t = lax.broadcasted_iota(jnp.int32, (rows, TOK), 0) + part * rows
                        k = lax.broadcasted_iota(jnp.int32, (rows, TOK), 1)
                        ex = jnp.where(k > t if mode == 1 else k <= t, ex, 0.0)
                    eb = ex.astype(BF16)
                    eg_ref[u, 0, h, at, :] = eb
                    eg_ref[u, 1, h, at, :] = (ex * (1.0 - th * th)).astype(BF16)
                    acc[h, at, :] += ndot(eb, value)

        for want, mode in ((1, 1), (2, 2), (3, 0)):

            @pl.when(flag == want)
            def _():
                body(mode)

        return 0

    lax.fori_loop(0, PACK, one, 0)

    @pl.when(step == SLOTS // PACK - 1)
    def _():
        for h in range(2):
            inverse = 1.0 / acc[h, :, HD:]
            at_ref[:, h * HD : (h + 1) * HD] = (acc[h, :, :HD] * inverse).astype(BF16)
            li_ref[:, h * HD : (h + 1) * HD] = inverse
        row = lax.broadcasted_iota(jnp.int32, (2 * HD, 2 * HD), 0)
        col = lax.broadcasted_iota(jnp.int32, (2 * HD, 2 * HD), 1)
        core, left, plane, four, head = row // 128, (row // 64) % 2, (row // 8) % 8, (row // 2) % 4, row % 2
        source = head * HD + plane * 16 + left * 8 + core * 4 + four
        pick = jnp.where(col == source, 1.0, 0.0).astype(BF16)
        pt_ref[...] = tdot(pick, at_ref[...]).astype(BF16)


def forward(info, queries, cosf, sinf, panels):
    whole = lambda *shape: pl.BlockSpec(shape, lambda i, *_: (0,) * len(shape))
    sds = jax.ShapeDtypeStruct
    eg = pl.BlockSpec((PACK, 2, 2, TOK, TOK), lambda i, f: (i, 0, 0, 0, 0))
    return pl.pallas_call(
        forward_kernel,
        out_shape=(
            sds((SLOTS, 2, 2, TOK, TOK), BF16),
            sds((TOK, 2 * HD), BF16),
            sds((TOK, 2 * HD), BF16),
            sds((TOK, 2 * HD), F32),
            sds((2 * HD, TOK), BF16),
        ),
        grid_spec=pltpu.PrefetchScalarGridSpec(
            num_scalar_prefetch=1,
            grid=(SLOTS // PACK,),
            in_specs=[
                whole(TOK, 2 * HD),
                whole(TOK, HD),
                whole(TOK, HD),
                *([pl.BlockSpec((1, 2, TOK, HD), lambda i, f: (i // (4 // PACK), 0, 0, 0))] * 4),
            ],
            out_specs=(
                eg,
                whole(TOK, 2 * HD),
                whole(TOK, 2 * HD),
                whole(TOK, 2 * HD),
                whole(2 * HD, TOK),
            ),
            scratch_shapes=[pltpu.VMEM((2, TOK, 2 * HD), F32), pltpu.VMEM((2, TOK, HD), BF16)],
        ),
        compiler_params=pltpu.CompilerParams(dimension_semantics=("arbitrary",), vmem_limit_bytes=46 << 20),
        cost_estimate=pl.CostEstimate(flops=10_000_000_000, bytes_accessed=24_000_000, transcendentals=10_000_000),
        name="attend",
    )(info, queries, cosf, sinf, *panels)


CARRY = (
    ((HALF, 2 * HD), BF16),
    ((2, HALF, HD), F32),
    ((2, HD, HALF), BF16),
    ((2, HD, HALF), BF16),
    ((2, HALF, HD), F32),
)


def stack_rows(info, cots, first, cs):
    for d, ref in enumerate(cots):
        row = pl.multiple_of(first + lax.rem(info[2] + d, 4) * 64, 64)
        cs[pl.ds(row, 64), :] = ref[...]


def prepare(full, q_ref, at_ref, li_ref, do, dl, qt, dt):
    do[...] = full.astype(BF16)
    for h in range(2):
        col = slice(h * HD, (h + 1) * HD)
        grad = full[:, col].astype(BF16).astype(F32)
        inverse = li_ref[:, col]
        total = jnp.sum(grad * at_ref[:, col].astype(F32), axis=1, keepdims=True)
        dl[h] = jnp.broadcast_to(total, (HALF, HD))
        dt[h] = (grad * inverse).T.astype(BF16)
        qt[h] = (q_ref[:, col].astype(F32) * (inverse * QUERY_MULTIPLIER)).T.astype(BF16)


def backward_kernel(base, count, has_cots, has_prev, final, info, *refs):
    refs = list(refs)
    take = lambda n: [refs.pop(0) for _ in range(n)]
    cots = take(5) if has_cots else []
    carry_in = [] if has_cots else take(4 if base == 0 else 5)
    q_ref, at_ref = take(2) if has_cots else (None, None)
    li_ref = take(1)[0] if has_cots or final else None
    cos_ref, sin_ref = take(2) if final else (None, None)
    pairs = take(4)
    (eg_ref,) = take(1)
    if has_prev:
        (prev_ref,) = take(1)
        if final:
            take(1)
        keep_ref, send_ref = take(2)
    else:
        (part_ref,) = take(1)
    qg_ref = take(1)[0] if final else None
    carry_out = [] if final else take(1)
    cs, do, dl, qt, dt, dq, pair = refs
    if not has_cots:
        do, dl, qt, dt = carry_in[:4]
    step = pl.program_id(0)

    @pl.when(step == 0)
    def _():
        if has_cots:
            stack_rows(info, cots[:4], 0, cs)
            prepare(tdot(cs[...], cots[4][...]), q_ref, at_ref, li_ref, do, dl, qt, dt)
        if base == 0:
            dq[...] = jnp.zeros_like(dq)
        else:
            dq[...] = carry_in[4][...]

    def one(u, _):
        slot = base + step * PACK + u
        place = place_of(info, slot)
        flag = flag_of(info, slot)

        def put(dk, dv):
            if not has_prev:
                part_ref[u, 0] = dk
                part_ref[u, 1] = dv
                return

            @pl.when(place < 2)
            def _():
                keep_ref[place, 0] = dk
                keep_ref[place, 1] = dv

            @pl.when(place >= 2)
            def _():
                send_ref[place - 2, 0] = dk
                send_ref[place - 2, 1] = dv

        @pl.when(flag > 0)
        def _():
            load_pair(place, pairs, pair)
            key = pair[0]
            value = pair[1]
            dk = jnp.zeros((HD, TOK), F32)
            dv = jnp.zeros((HD, TOK), F32)
            for h in range(2):
                dp = tdot(do[:, h * HD : (h + 1) * HD], value)
                x = (eg_ref[u, 1, h].astype(F32) * (dp - dl[h][:, :1])).astype(BF16)
                dq[h] += ndot(x, key)
                dk += ndot(qt[h], x)
                dv += ndot(dt[h], eg_ref[u, 0, h])
            if has_prev:
                dk = dk + prev_ref[u, 0].astype(F32)
                dv = dv + prev_ref[u, 1].astype(F32)
            put(dk.astype(BF16), dv.astype(BF16))

        if has_prev:

            @pl.when(flag == 0)
            def _():
                zero = jnp.zeros((HD, TOK), BF16)
                put(zero, zero)

        return 0

    lax.fori_loop(0, PACK, one, 0)

    @pl.when(step == count // PACK - 1)
    def _():
        if final:
            cosine = cos_ref[...]
            sine = sin_ref[...]
            for h in range(2):
                col = slice(h * HD, (h + 1) * HD)
                g = dq[h] * (li_ref[:, col] * QUERY_MULTIPLIER)
                qg_ref[:, col] = g * cosine - pltpu.roll(g, HD // 2, 1) * sine
        else:
            carry_out[0][...] = dq[...]


def backward(base, count, which, info, rows, panels, eg_all, cots=None, w2=None, carry=None, prev=None, grad=None):
    has_cots, has_prev = cots is not None, prev is not None
    final = base + count == SLOTS
    sds = jax.ShapeDtypeStruct
    whole = lambda *shape: pl.BlockSpec(shape, lambda i, *_: (0,) * len(shape))
    tok = lambda width: pl.BlockSpec((HALF, width), lambda i, f: (half_of(f, which), 0))
    eg = pl.BlockSpec((PACK, 2, 2, HALF, TOK), lambda i, f: (base // PACK + i, 0, 0, half_of(f, which), 0))
    part = pl.BlockSpec((PACK, 2, HD, TOK), lambda i, f: (base // PACK + i, 0, 0, 0))
    ins, args, alias = [], [], {}
    if has_cots:
        ins += [whole(64, 4608)] * 4 + [whole(2 * HD, 4608)]
        args += [*cots, w2]
    else:
        ins += [whole(*shape) for shape, _ in CARRY[: len(carry)]]
        args += list(carry)
    wanted = [has_cots, has_cots, has_cots or final, final, final]
    widths = [2 * HD, 2 * HD, 2 * HD, HD, HD]
    ins += [tok(n) for n, use in zip(widths, wanted) if use]
    args += [a for a, use in zip(rows, wanted) if use]
    ins += [pl.BlockSpec((1, 2, TOK, HD), lambda i, f: (base // 4 + i // (4 // PACK), 0, 0, 0))] * 4 + [eg]
    args += [*panels, eg_all]
    if has_prev:
        ins += [part]
        args += [prev]
        outs = [whole(2, 2, HD, TOK)] * 2
        shapes = [sds((2, 2, HD, TOK), BF16)] * 2
    else:
        outs = [part]
        shapes = [sds((SLOTS, 2, HD, TOK), BF16)]
    if final:
        if grad is not None:
            ins += [pl.BlockSpec(memory_space=pl.ANY)]
            args += [grad]
            alias = {len(args): len(outs)}
        outs += [tok(2 * HD)]
        shapes += [sds((TOK, 2 * HD), F32)]
    else:
        outs += [whole(*CARRY[4][0])]
        shapes += [sds(*CARRY[4])]

    def kernel(*refs):
        backward_kernel(base, count, has_cots, has_prev, final, *refs)

    return pl.pallas_call(
        kernel,
        out_shape=shapes,
        grid_spec=pltpu.PrefetchScalarGridSpec(
            num_scalar_prefetch=1,
            grid=(count // PACK,),
            in_specs=ins,
            out_specs=outs,
            scratch_shapes=[
                pltpu.VMEM((HALF, 4608) if has_cots else (16, 128), BF16),
                *(pltpu.VMEM(*c) for c in CARRY),
                pltpu.VMEM((2, TOK, HD), BF16),
            ],
        ),
        compiler_params=pltpu.CompilerParams(dimension_semantics=("arbitrary",), vmem_limit_bytes=(60 if has_prev else 46) << 20),
        input_output_aliases=alias,
        cost_estimate=pl.CostEstimate(flops=700_000_000 * count, bytes_accessed=2_000_000 * count, transcendentals=0),
    )(info, *args)


def weight_kernel(info, *refs):
    cots = refs[:8]
    pt_ref, w_ref, q_ref, at_ref, li_ref, keep_ref, send_ref, do, dl, qt, dt, cs, full = refs[8:]
    own, core = info[3], info[4]
    near = pl.multiple_of(own * HALF, HALF)
    away = pl.multiple_of((1 - own) * HALF, HALF)
    stack_rows(info, cots[:4], near, cs)
    stack_rows(info, cots[4:], away, cs)
    rows = cs[...]
    mine = pl.multiple_of(core * HD, HD)
    other = pl.multiple_of((1 - core) * HD, HD)
    keep_ref[...] = ndot(pt_ref[pl.ds(mine, HD), :], rows)
    send_ref[...] = ndot(pt_ref[pl.ds(other, HD), :], rows).astype(BF16)
    part = tdot(cs[pl.ds(away, HALF), :], w_ref[...])

    @pl.when(pl.program_id(0) == 0)
    def _():
        full[...] = part

    @pl.when(pl.program_id(0) > 0)
    def _():
        full[...] += part

    @pl.when(pl.program_id(0) == pl.num_programs(0) - 1)
    def _():
        prepare(full[...], q_ref, at_ref, li_ref, do, dl, qt, dt)


def weight(info, cots, attn_t, w2, rows):
    chunk = 1152
    sds = jax.ShapeDtypeStruct
    block = lambda n: pl.BlockSpec((n, chunk), lambda i, f: (0, i))
    whole = lambda *shape: pl.BlockSpec(shape, lambda i, *_: (0,) * len(shape))
    tok = pl.BlockSpec((HALF, 2 * HD), lambda i, f: (1 - f[3], 0))
    return pl.pallas_call(
        weight_kernel,
        out_shape=(sds((HD, 4608), F32), sds((HD, 4608), BF16), *(sds(*c) for c in CARRY[:4])),
        grid_spec=pltpu.PrefetchScalarGridSpec(
            num_scalar_prefetch=1,
            grid=(4608 // chunk,),
            in_specs=[block(64)] * 8 + [whole(2 * HD, TOK), block(2 * HD), tok, tok, tok],
            out_specs=(block(HD), block(HD), *(whole(*shape) for shape, _ in CARRY[:4])),
            scratch_shapes=[pltpu.VMEM((TOK, chunk), BF16), pltpu.VMEM((HALF, 2 * HD), F32)],
        ),
        compiler_params=pltpu.CompilerParams(dimension_semantics=("arbitrary",), vmem_limit_bytes=60 << 20),
        cost_estimate=pl.CostEstimate(flops=1_900_000_000, bytes_accessed=11_000_000, transcendentals=0),
        name="weigh",
    )(info, *cots, attn_t, w2, *rows[:3])


def settle_kernel(own_ref, left_ref, down_ref, cos_ref, sin_ref, kg_ref, vg_ref):
    both = own_ref[0] + left_ref[...].astype(F32) + down_ref[...].astype(F32)
    g = both[0].T
    kg_ref[...] = g * cos_ref[...] - pltpu.roll(g, HD // 2, 1) * sin_ref[...]
    vg_ref[...] = both[1].T


def settle(both, left, down, cosf, sinf):
    whole = lambda *shape: pl.BlockSpec(shape, lambda i, *_: (0,) * len(shape))
    sds = jax.ShapeDtypeStruct
    return pl.pallas_call(
        settle_kernel,
        out_shape=(sds((TOK, HD), F32), sds((TOK, HD), F32)),
        grid=(1,),
        in_specs=[whole(1, 2, HD, TOK), whole(2, HD, TOK), whole(2, HD, TOK), whole(TOK, HD), whole(TOK, HD)],
        out_specs=(whole(TOK, HD), whole(TOK, HD)),
        compiler_params=pltpu.CompilerParams(dimension_semantics=("arbitrary",), vmem_limit_bytes=46 << 20),
        cost_estimate=pl.CostEstimate(flops=500_000, bytes_accessed=2_000_000, transcendentals=0),
        name="settle",
    )(both, left, down, cosf, sinf)


def local(queries, keys, values, out_weight, cotangent):
    z, xl, c = (lax.axis_index(a) for a in CTX)
    xh, y = (lax.axis_index(a) for a in HEAD)
    lane = xl * 2 + c
    ctx = z * 4 + lane
    cosf, sinf = tables(ctx * TOK)

    info = jnp.stack([lane, ctx, y, xh, c]).astype(jnp.int32)

    own = turn(keys, values, cosf, sinf)
    behind1 = along_z(own, 1)
    behind2 = along_z(own, 2)
    across0 = swap(own, "xl")
    near1 = from_y(cotangent, 1)
    near3 = from_y(cotangent, 3)
    far0 = swap(cotangent, "xh")
    near2 = from_y(cotangent, 2)
    near = [cotangent, near1, near2, near3]
    far = [far0]
    for d in (1, 2, 3):
        far.append(from_y(far0, d))
    back = jnp.concatenate([behind2, behind1])
    across = swap(back, "xl")
    mine = jnp.concatenate([back, own])
    partner1 = swap(mine, "c")
    across = jnp.concatenate([across, across0])
    partner2 = swap(across, "c")
    panels = (mine, across, partner1, partner2)

    w2 = jnp.transpose(out_weight, (1, 0, 2)).reshape(2 * HD, 4608)

    eg, qr, attn, linv, attn_t = forward(info, queries, cosf, sinf, panels)
    rows = (qr, attn, linv, cosf, sinf)
    prev, half = backward(0, SLOTS, 1, info, rows, panels, eg, cots=near, w2=w2)

    wkeep, wsend, *carry = weight(info, near + far, attn_t, w2, rows)
    wgot = swap(wsend, "c")
    wkeep, wgot = wkeep.reshape(2, 64, 4608), wgot.reshape(2, 64, 4608)
    half_at = lambda a, n: lax.dynamic_index_in_dim(a, n, 0, False).astype(F32)
    wgive = (half_at(wkeep, 1 - xl) + half_at(wgot, 1 - xl)).astype(BF16)
    wback = swap(wgive, "xl")
    wz = (half_at(wkeep, xl) + half_at(wgot, xl) + wback.astype(F32)).astype(BF16).reshape(8, 8, 4608)
    wz = lax.all_to_all(wz, "z", 0, 0, tiled=True)
    weight_grad = jnp.sum(wz.astype(F32), axis=0).reshape(4, 2, 4608)

    total = []
    for p in range(PANELS):
        out = backward(
            p * 4, 4, 2, info, rows, panels, eg,
            carry=carry, prev=prev, grad=half if p == PANELS - 1 else None,
        )
        keep, send, last = out
        carry = [*carry[:4], last]
        got = swap(send, "c")
        both = keep.astype(F32) + got.astype(F32)
        give = both[1].astype(BF16)
        turned = swap(give, "xl")
        total.append((both, turned))
    query_grad = last
    down1 = along_z((total[0][0][0] + total[0][1].astype(F32)).astype(BF16), -1)
    down0 = along_z((total[1][0][0] + total[1][1].astype(F32) + down1.astype(F32)).astype(BF16), -1)
    key_grad, value_grad = settle(*total[2], down0, cosf, sinf)
    return query_grad, key_grad, value_grad, weight_grad


def solution(mesh):
    fine = Mesh(mesh.devices.reshape(8, 2, 2, 2, 4), CTX + HEAD)
    placed = (P(CTX, HEAD), P(CTX, HEAD), P(CTX, HEAD), P(None, HEAD, None), P(CTX + HEAD, None))
    return jax.shard_map(
        local,
        mesh=fine,
        in_specs=placed,
        out_specs=(P(CTX, HEAD), P(CTX, HEAD), P(CTX, HEAD), P(CTX, HEAD, None)),
        check_vma=False,
    )
```

```python
import jax
import jax.numpy as jnp
import numpy as np
from jax import lax
from jax.experimental import pallas as pl
from jax.experimental.pallas import tpu as pltpu
from jax.sharding import Mesh, PartitionSpec as P

SOFT_CAP = 50.0
QUERY_MULTIPLIER = 144.0 ** (-0.5)
ROPE_BASE = 10000.0
LOG2E = 1.4426950408889634
CTX = ("z", "xl", "c")
HEAD = ("xh", "y")
TOK = 512
HALF = 256
HD = 128
PANELS = 3
SLOTS = 12
TILES = 9
PACK = 2
NT = (((1,), (1,)), ((), ()))
F32 = jnp.float32
BF16 = jnp.bfloat16


def permute(x, axis, pairs):
    return lax.ppermute(x, axis, pairs)


def from_y(x, d):
    return permute(x, "y", [((i + d) % 4, i) for i in range(4)])


def swap(x, axis):
    return permute(x, axis, [(0, 1), (1, 0)])


def along_z(x, step):
    return permute(x, "z", [(i, i + step) for i in range(8) if 0 <= i + step < 8])


FREQUENCY = np.asarray([ROPE_BASE ** (-2.0 * (n % (HD // 2)) / HD) for n in range(HD)], np.float32)
SIGN = np.asarray([-1.0 if n < HD // 2 else 1.0 for n in range(HD)], np.float32)


def tables(first_row):
    positions = first_row + jnp.arange(TOK, dtype=jnp.int32)
    angles = positions.astype(F32)[:, None] * FREQUENCY[None, :]
    return jnp.cos(angles), SIGN[None, :] * jnp.sin(angles)


def place_of(info, i):
    rel = (i & 3) ^ info[0]
    return ((rel & 1) << 1) | (rel >> 1)


def flag_of(info, i):
    index = i - info[0]
    valid = (index >= 0) & (index < TILES) & (info[1] - (TILES - 1) + index >= 0)
    return jnp.where(valid, jnp.where(index == 0, 1, jnp.where(index == TILES - 1, 2, 3)), 0)


def half_of(info, which):
    return info[3] if which == 1 else 1 - info[3]


def ndot(a, b):
    return jnp.dot(a, b, preferred_element_type=F32)


def tdot(a, b):
    return lax.dot_general(a, b, NT, preferred_element_type=F32)


def turn_kernel(k_ref, v_ref, cos_ref, sin_ref, own_ref):
    x = k_ref[...].astype(F32)
    own_ref[0, 0] = (x * cos_ref[...] + pltpu.roll(x, HD // 2, 1) * sin_ref[...]).astype(BF16)
    own_ref[0, 1] = v_ref[...]


def turn(keys, values, cosf, sinf):
    whole = lambda *shape: pl.BlockSpec(shape, lambda i, *_: (0,) * len(shape))
    return pl.pallas_call(
        turn_kernel,
        out_shape=jax.ShapeDtypeStruct((1, 2, TOK, HD), BF16),
        grid=(1,),
        in_specs=[whole(TOK, HD)] * 4,
        out_specs=whole(1, 2, TOK, HD),
        compiler_params=pltpu.CompilerParams(dimension_semantics=("arbitrary",), vmem_limit_bytes=46 << 20),
        cost_estimate=pl.CostEstimate(flops=500_000, bytes_accessed=1_000_000, transcendentals=0),
        name="turn",
    )(keys, values, cosf, sinf)


def load_pair(place, refs, pair):
    for n, ref in enumerate(refs):

        @pl.when(place == n)
        def _():
            pair[...] = ref[0]


def forward_kernel(
    info, qr_ref, r0, r2, r1, r3, eg_ref, at_ref, li_ref, pt_ref, acc, pair
):
    step = pl.program_id(0)

    @pl.when(step == 0)
    def _():
        acc[...] = jnp.zeros_like(acc)

    def one(u, _):
        slot = step * PACK + u
        flag = flag_of(info, slot)

        @pl.when(flag > 0)
        def _():
            load_pair(place_of(info, slot), (r0, r2, r1, r3), pair)

        def body(mode):
            key = pair[0]
            value = jnp.concatenate([pair[1], jnp.ones((TOK, HD), BF16)], axis=1)
            rows = HALF
            for h in range(2):
                for part in range(TOK // rows):
                    at = pl.ds(part * rows, rows)
                    s = tdot(qr_ref[at, h * HD : (h + 1) * HD], key)
                    th = jnp.tanh(s * (QUERY_MULTIPLIER / SOFT_CAP))
                    ex = jnp.exp2(th * (SOFT_CAP * LOG2E))
                    if mode:
                        t = lax.broadcasted_iota(jnp.int32, (rows, TOK), 0) + part * rows
                        k = lax.broadcasted_iota(jnp.int32, (rows, TOK), 1)
                        ex = jnp.where(k > t if mode == 1 else k <= t, ex, 0.0)
                    eb = ex.astype(BF16)
                    eg_ref[u, 0, h, at, :] = eb
                    eg_ref[u, 1, h, at, :] = (ex * (1.0 - th * th)).astype(BF16)
                    acc[h, at, :] += ndot(eb, value)

        for want, mode in ((1, 1), (2, 2), (3, 0)):

            @pl.when(flag == want)
            def _():
                body(mode)

        return 0

    lax.fori_loop(0, PACK, one, 0)

    @pl.when(step == SLOTS // PACK - 1)
    def _():
        for h in range(2):
            inverse = 1.0 / acc[h, :, HD:]
            at_ref[:, h * HD : (h + 1) * HD] = (acc[h, :, :HD] * inverse).astype(BF16)
            li_ref[:, h * HD : (h + 1) * HD] = inverse
        row = lax.broadcasted_iota(jnp.int32, (2 * HD, 2 * HD), 0)
        col = lax.broadcasted_iota(jnp.int32, (2 * HD, 2 * HD), 1)
        core, left, plane, four, head = row // 128, (row // 64) % 2, (row // 8) % 8, (row // 2) % 4, row % 2
        source = head * HD + plane * 16 + left * 8 + core * 4 + four
        pick = jnp.where(col == source, 1.0, 0.0).astype(BF16)
        pt_ref[...] = tdot(pick, at_ref[...]).astype(BF16)


def spin_kernel(q_ref, cos_ref, sin_ref, qr_ref):
    for h in range(2):
        col = slice(h * HD, (h + 1) * HD)
        x = q_ref[:, col].astype(F32)
        qr_ref[:, col] = (x * cos_ref[...] + pltpu.roll(x, HD // 2, 1) * sin_ref[...]).astype(BF16)


def spin(queries, cosf, sinf):
    whole = lambda *shape: pl.BlockSpec(shape, lambda i, *_: (0,) * len(shape))
    return pl.pallas_call(
        spin_kernel,
        out_shape=jax.ShapeDtypeStruct((TOK, 2 * HD), BF16),
        grid=(1,),
        in_specs=[whole(TOK, 2 * HD), whole(TOK, HD), whole(TOK, HD)],
        out_specs=whole(TOK, 2 * HD),
        compiler_params=pltpu.CompilerParams(dimension_semantics=("arbitrary",), vmem_limit_bytes=60 << 20),
        cost_estimate=pl.CostEstimate(flops=500_000, bytes_accessed=1_000_000, transcendentals=0),
        name="spin",
    )(queries, cosf, sinf)


def forward(info, qr, panels):
    whole = lambda *shape: pl.BlockSpec(shape, lambda i, *_: (0,) * len(shape))
    sds = jax.ShapeDtypeStruct
    eg = pl.BlockSpec((PACK, 2, 2, TOK, TOK), lambda i, f: (i, 0, 0, 0, 0))
    return pl.pallas_call(
        forward_kernel,
        out_shape=(
            sds((SLOTS, 2, 2, TOK, TOK), BF16),
            sds((TOK, 2 * HD), BF16),
            sds((TOK, 2 * HD), F32),
            sds((2 * HD, TOK), BF16),
        ),
        grid_spec=pltpu.PrefetchScalarGridSpec(
            num_scalar_prefetch=1,
            grid=(SLOTS // PACK,),
            in_specs=[
                whole(TOK, 2 * HD),
                *([pl.BlockSpec((1, 2, TOK, HD), lambda i, f: (i // (4 // PACK), 0, 0, 0))] * 4),
            ],
            out_specs=(
                eg,
                whole(TOK, 2 * HD),
                whole(TOK, 2 * HD),
                whole(2 * HD, TOK),
            ),
            scratch_shapes=[pltpu.VMEM((2, TOK, 2 * HD), F32), pltpu.VMEM((2, TOK, HD), BF16)],
        ),
        compiler_params=pltpu.CompilerParams(dimension_semantics=("arbitrary",), vmem_limit_bytes=46 << 20),
        cost_estimate=pl.CostEstimate(flops=10_000_000_000, bytes_accessed=24_000_000, transcendentals=10_000_000),
        name="attend",
    )(info, qr, *panels)


CARRY = (
    ((HALF, 2 * HD), BF16),
    ((2, HALF, HD), F32),
    ((2, HD, HALF), BF16),
    ((2, HD, HALF), BF16),
    ((2, HALF, HD), F32),
)


def stack_rows(info, cots, first, cs):
    for d, ref in enumerate(cots):
        row = pl.multiple_of(first + lax.rem(info[2] + d, 4) * 64, 64)
        cs[pl.ds(row, 64), :] = ref[...]


def prepare(full, q_ref, at_ref, li_ref, do, dl, qt, dt):
    do[...] = full.astype(BF16)
    for h in range(2):
        col = slice(h * HD, (h + 1) * HD)
        grad = full[:, col].astype(BF16).astype(F32)
        inverse = li_ref[:, col]
        total = jnp.sum(grad * at_ref[:, col].astype(F32), axis=1, keepdims=True)
        dl[h] = jnp.broadcast_to(total, (HALF, HD))
        dt[h] = (grad * inverse).T.astype(BF16)
        qt[h] = (q_ref[:, col].astype(F32) * (inverse * QUERY_MULTIPLIER)).T.astype(BF16)


def backward_kernel(base, count, has_cots, has_prev, final, info, *refs):
    refs = list(refs)
    take = lambda n: [refs.pop(0) for _ in range(n)]
    cots = take(5) if has_cots else []
    carry_in = [] if has_cots else take(4 if base == 0 else 5)
    q_ref, at_ref = take(2) if has_cots else (None, None)
    li_ref = take(1)[0] if has_cots or final else None
    cos_ref, sin_ref = take(2) if final else (None, None)
    pairs = take(4)
    (eg_ref,) = take(1)
    if has_prev:
        (prev_ref,) = take(1)
        if final:
            take(1)
        keep_ref, send_ref = take(2)
    else:
        (part_ref,) = take(1)
    qg_ref = take(1)[0] if final else None
    carry_out = [] if final else take(1)
    cs, do, dl, qt, dt, dq, pair = refs
    if not has_cots:
        do, dl, qt, dt = carry_in[:4]
    step = pl.program_id(0)

    @pl.when(step == 0)
    def _():
        if has_cots:
            stack_rows(info, cots[:4], 0, cs)
            prepare(tdot(cs[...], cots[4][...]), q_ref, at_ref, li_ref, do, dl, qt, dt)
        if base == 0:
            dq[...] = jnp.zeros_like(dq)
        else:
            dq[...] = carry_in[4][...]

    def one(u, _):
        slot = base + step * PACK + u
        place = place_of(info, slot)
        flag = flag_of(info, slot)

        def put(dk, dv):
            if not has_prev:
                part_ref[u, 0] = dk
                part_ref[u, 1] = dv
                return

            @pl.when(place < 2)
            def _():
                keep_ref[place, 0] = dk
                keep_ref[place, 1] = dv

            @pl.when(place >= 2)
            def _():
                send_ref[place - 2, 0] = dk
                send_ref[place - 2, 1] = dv

        @pl.when(flag > 0)
        def _():
            load_pair(place, pairs, pair)
            key = pair[0]
            value = pair[1]
            dk = jnp.zeros((HD, TOK), F32)
            dv = jnp.zeros((HD, TOK), F32)
            for h in range(2):
                dp = tdot(do[:, h * HD : (h + 1) * HD], value)
                x = (eg_ref[u, 1, h].astype(F32) * (dp - dl[h][:, :1])).astype(BF16)
                dq[h] += ndot(x, key)
                dk += ndot(qt[h], x)
                dv += ndot(dt[h], eg_ref[u, 0, h])
            if has_prev:
                dk = dk + prev_ref[u, 0].astype(F32)
                dv = dv + prev_ref[u, 1].astype(F32)
            put(dk.astype(BF16), dv.astype(BF16))

        if has_prev:

            @pl.when(flag == 0)
            def _():
                zero = jnp.zeros((HD, TOK), BF16)
                put(zero, zero)

        return 0

    lax.fori_loop(0, PACK, one, 0)

    @pl.when(step == count // PACK - 1)
    def _():
        if final:
            cosine = cos_ref[...]
            sine = sin_ref[...]
            for h in range(2):
                col = slice(h * HD, (h + 1) * HD)
                g = dq[h] * (li_ref[:, col] * QUERY_MULTIPLIER)
                qg_ref[:, col] = g * cosine - pltpu.roll(g, HD // 2, 1) * sine
        else:
            carry_out[0][...] = dq[...]


def backward(base, count, which, info, rows, panels, eg_all, cots=None, w2=None, carry=None, prev=None, grad=None):
    has_cots, has_prev = cots is not None, prev is not None
    final = base + count == SLOTS
    sds = jax.ShapeDtypeStruct
    whole = lambda *shape: pl.BlockSpec(shape, lambda i, *_: (0,) * len(shape))
    tok = lambda width: pl.BlockSpec((HALF, width), lambda i, f: (half_of(f, which), 0))
    eg = pl.BlockSpec((PACK, 2, 2, HALF, TOK), lambda i, f: (base // PACK + i, 0, 0, half_of(f, which), 0))
    part = pl.BlockSpec((PACK, 2, HD, TOK), lambda i, f: (base // PACK + i, 0, 0, 0))
    ins, args, alias = [], [], {}
    if has_cots:
        ins += [whole(64, 4608)] * 4 + [whole(2 * HD, 4608)]
        args += [*cots, w2]
    else:
        ins += [whole(*shape) for shape, _ in CARRY[: len(carry)]]
        args += list(carry)
    wanted = [has_cots, has_cots, has_cots or final, final, final]
    widths = [2 * HD, 2 * HD, 2 * HD, HD, HD]
    ins += [tok(n) for n, use in zip(widths, wanted) if use]
    args += [a for a, use in zip(rows, wanted) if use]
    ins += [pl.BlockSpec((1, 2, TOK, HD), lambda i, f: (base // 4 + i // (4 // PACK), 0, 0, 0))] * 4 + [eg]
    args += [*panels, eg_all]
    if has_prev:
        ins += [part]
        args += [prev]
        outs = [whole(2, 2, HD, TOK)] * 2
        shapes = [sds((2, 2, HD, TOK), BF16)] * 2
    else:
        outs = [part]
        shapes = [sds((SLOTS, 2, HD, TOK), BF16)]
    if final:
        if grad is not None:
            ins += [pl.BlockSpec(memory_space=pl.ANY)]
            args += [grad]
            alias = {len(args): len(outs)}
        outs += [tok(2 * HD)]
        shapes += [sds((TOK, 2 * HD), F32)]
    else:
        outs += [whole(*CARRY[4][0])]
        shapes += [sds(*CARRY[4])]

    def kernel(*refs):
        backward_kernel(base, count, has_cots, has_prev, final, *refs)

    return pl.pallas_call(
        kernel,
        out_shape=shapes,
        grid_spec=pltpu.PrefetchScalarGridSpec(
            num_scalar_prefetch=1,
            grid=(count // PACK,),
            in_specs=ins,
            out_specs=outs,
            scratch_shapes=[
                pltpu.VMEM((HALF, 4608) if has_cots else (16, 128), BF16),
                *(pltpu.VMEM(*c) for c in CARRY),
                pltpu.VMEM((2, TOK, HD), BF16),
            ],
        ),
        compiler_params=pltpu.CompilerParams(dimension_semantics=("arbitrary",), vmem_limit_bytes=(60 if has_prev else 46) << 20),
        input_output_aliases=alias,
        cost_estimate=pl.CostEstimate(flops=700_000_000 * count, bytes_accessed=2_000_000 * count, transcendentals=0),
    )(info, *args)


def weight_kernel(info, *refs):
    cots = refs[:8]
    pt_ref, w_ref, q_ref, at_ref, li_ref, keep_ref, send_ref, do, dl, qt, dt, cs, full = refs[8:]
    own, core = info[3], info[4]
    near = pl.multiple_of(own * HALF, HALF)
    away = pl.multiple_of((1 - own) * HALF, HALF)
    stack_rows(info, cots[:4], near, cs)
    stack_rows(info, cots[4:], away, cs)
    rows = cs[...]
    mine = pl.multiple_of(core * HD, HD)
    other = pl.multiple_of((1 - core) * HD, HD)
    both = ndot(jnp.concatenate([pt_ref[pl.ds(mine, HD), :], pt_ref[pl.ds(other, HD), :]]), rows)
    keep_ref[...] = both[:HD]
    send_ref[...] = both[HD:].astype(BF16)
    part = tdot(cs[pl.ds(away, HALF), :], w_ref[...])

    @pl.when(pl.program_id(0) == 0)
    def _():
        full[...] = part

    @pl.when(pl.program_id(0) > 0)
    def _():
        full[...] += part

    @pl.when(pl.program_id(0) == pl.num_programs(0) - 1)
    def _():
        prepare(full[...], q_ref, at_ref, li_ref, do, dl, qt, dt)


def weight(info, cots, attn_t, w2, rows):
    chunk = 2304
    sds = jax.ShapeDtypeStruct
    block = lambda n: pl.BlockSpec((n, chunk), lambda i, f: (0, i))
    whole = lambda *shape: pl.BlockSpec(shape, lambda i, *_: (0,) * len(shape))
    tok = pl.BlockSpec((HALF, 2 * HD), lambda i, f: (1 - f[3], 0))
    return pl.pallas_call(
        weight_kernel,
        out_shape=(sds((HD, 4608), F32), sds((HD, 4608), BF16), *(sds(*c) for c in CARRY[:4])),
        grid_spec=pltpu.PrefetchScalarGridSpec(
            num_scalar_prefetch=1,
            grid=(4608 // chunk,),
            in_specs=[block(64)] * 8 + [whole(2 * HD, TOK), block(2 * HD), tok, tok, tok],
            out_specs=(block(HD), block(HD), *(whole(*shape) for shape, _ in CARRY[:4])),
            scratch_shapes=[pltpu.VMEM((TOK, chunk), BF16), pltpu.VMEM((HALF, 2 * HD), F32)],
        ),
        compiler_params=pltpu.CompilerParams(dimension_semantics=("arbitrary",), vmem_limit_bytes=60 << 20),
        cost_estimate=pl.CostEstimate(flops=1_900_000_000, bytes_accessed=11_000_000, transcendentals=0),
        name="weigh",
    )(info, *cots, attn_t, w2, *rows[:3])


def settle_kernel(own_ref, left_ref, down_ref, cos_ref, sin_ref, kg_ref, vg_ref):
    both = own_ref[0] + left_ref[...].astype(F32) + down_ref[...].astype(F32)
    g = both[0].T
    kg_ref[...] = g * cos_ref[...] - pltpu.roll(g, HD // 2, 1) * sin_ref[...]
    vg_ref[...] = both[1].T


def settle(both, left, down, cosf, sinf):
    whole = lambda *shape: pl.BlockSpec(shape, lambda i, *_: (0,) * len(shape))
    sds = jax.ShapeDtypeStruct
    return pl.pallas_call(
        settle_kernel,
        out_shape=(sds((TOK, HD), F32), sds((TOK, HD), F32)),
        grid=(1,),
        in_specs=[whole(1, 2, HD, TOK), whole(2, HD, TOK), whole(2, HD, TOK), whole(TOK, HD), whole(TOK, HD)],
        out_specs=(whole(TOK, HD), whole(TOK, HD)),
        compiler_params=pltpu.CompilerParams(dimension_semantics=("arbitrary",), vmem_limit_bytes=46 << 20),
        cost_estimate=pl.CostEstimate(flops=500_000, bytes_accessed=2_000_000, transcendentals=0),
        name="settle",
    )(both, left, down, cosf, sinf)


def local(queries, keys, values, out_weight, cotangent):
    z, xl, c = (lax.axis_index(a) for a in CTX)
    xh, y = (lax.axis_index(a) for a in HEAD)
    lane = xl * 2 + c
    ctx = z * 4 + lane
    cosf, sinf = tables(ctx * TOK)

    info = jnp.stack([lane, ctx, y, xh, c]).astype(jnp.int32)

    own = turn(keys, values, cosf, sinf)
    behind1 = along_z(own, 1)
    behind2 = along_z(own, 2)
    across0 = swap(own, "xl")
    near1 = from_y(cotangent, 1)
    near3 = from_y(cotangent, 3)
    far0 = swap(cotangent, "xh")
    near2 = from_y(cotangent, 2)
    near = [cotangent, near1, near2, near3]
    far = [far0]
    for d in (1, 2, 3):
        far.append(from_y(far0, d))
    beside1 = along_z(across0, 1)
    across = swap(behind2, "xl")
    mine = jnp.concatenate([behind2, behind1, own])
    partner1 = swap(mine, "c")
    across = jnp.concatenate([across, beside1, across0])
    partner2 = swap(across, "c")
    panels = (mine, across, partner1, partner2)

    w2 = jnp.transpose(out_weight, (1, 0, 2)).reshape(2 * HD, 4608)

    qr = spin(queries, cosf, sinf)
    eg, attn, linv, attn_t = forward(info, qr, panels)
    rows = (qr, attn, linv, cosf, sinf)
    prev, half = backward(0, SLOTS, 1, info, rows, panels, eg, cots=near, w2=w2)

    wkeep, wsend, *carry = weight(info, near + far, attn_t, w2, rows)
    wgot = swap(wsend, "c")
    wkeep, wgot = wkeep.reshape(2, 64, 4608), wgot.reshape(2, 64, 4608)
    half_at = lambda a, n: lax.dynamic_index_in_dim(a, n, 0, False).astype(F32)
    wgive = (half_at(wkeep, 1 - xl) + half_at(wgot, 1 - xl)).astype(BF16)
    wback = swap(wgive, "xl")
    wz = (half_at(wkeep, xl) + half_at(wgot, xl) + wback.astype(F32)).astype(BF16).reshape(8, 8, 4608)
    wz = lax.all_to_all(wz, "z", 0, 0, tiled=True)
    weight_grad = jnp.sum(wz.astype(F32), axis=0).reshape(4, 2, 4608)

    total = []
    for p in range(PANELS):
        out = backward(
            p * 4, 4, 2, info, rows, panels, eg,
            carry=carry, prev=prev, grad=half if p == PANELS - 1 else None,
        )
        keep, send, last = out
        carry = [*carry[:4], last]
        got = swap(send, "c")
        both = keep.astype(F32) + got.astype(F32)
        give = both[1].astype(BF16)
        turned = swap(give, "xl")
        total.append((both, turned))
    query_grad = last
    down1 = along_z((total[0][0][0] + total[0][1].astype(F32)).astype(BF16), -1)
    down0 = along_z((total[1][0][0] + total[1][1].astype(F32) + down1.astype(F32)).astype(BF16), -1)
    key_grad, value_grad = settle(*total[2], down0, cosf, sinf)
    return query_grad, key_grad, value_grad, weight_grad


def solution(mesh):
    fine = Mesh(mesh.devices.reshape(8, 2, 2, 2, 4), CTX + HEAD)
    placed = (P(CTX, HEAD), P(CTX, HEAD), P(CTX, HEAD), P(None, HEAD, None), P(CTX + HEAD, None))
    return jax.shard_map(
        local,
        mesh=fine,
        in_specs=placed,
        out_specs=(P(CTX, HEAD), P(CTX, HEAD), P(CTX, HEAD), P(CTX, HEAD, None)),
        check_vma=False,
    )
```

```python
import jax
import jax.numpy as jnp
import numpy as np
from jax import lax
from jax.experimental import pallas as pl
from jax.experimental.pallas import tpu as pltpu
from jax.sharding import Mesh, PartitionSpec as P

SOFT_CAP = 50.0
QUERY_MULTIPLIER = 144.0 ** (-0.5)
ROPE_BASE = 10000.0
LOG2E = 1.4426950408889634
CTX = ("z", "xl", "c")
HEAD = ("xh", "y")
TOK = 512
HALF = 256
HD = 128
PANELS = 3
SLOTS = 12
TILES = 9
PACK = 2
NT = (((1,), (1,)), ((), ()))
F32 = jnp.float32
BF16 = jnp.bfloat16


def permute(x, axis, pairs):
    return lax.ppermute(x, axis, pairs)


def from_y(x, d):
    return permute(x, "y", [((i + d) % 4, i) for i in range(4)])


def swap(x, axis):
    return permute(x, axis, [(0, 1), (1, 0)])


def along_z(x, step):
    return permute(x, "z", [(i, i + step) for i in range(8) if 0 <= i + step < 8])


FREQUENCY = np.asarray([ROPE_BASE ** (-2.0 * (n % (HD // 2)) / HD) for n in range(HD)], np.float32)
SIGN = np.asarray([-1.0 if n < HD // 2 else 1.0 for n in range(HD)], np.float32)


def tables(first_row):
    positions = first_row + jnp.arange(TOK, dtype=jnp.int32)
    angles = positions.astype(F32)[:, None] * FREQUENCY[None, :]
    return jnp.cos(angles), SIGN[None, :] * jnp.sin(angles)


def place_of(info, i):
    rel = (i & 3) ^ info[0]
    return ((rel & 1) << 1) | (rel >> 1)


def flag_of(info, i):
    index = i - info[0]
    valid = (index >= 0) & (index < TILES) & (info[1] - (TILES - 1) + index >= 0)
    return jnp.where(valid, jnp.where(index == 0, 1, jnp.where(index == TILES - 1, 2, 3)), 0)


def half_of(info, which):
    return info[3] if which == 1 else 1 - info[3]


def ndot(a, b):
    return jnp.dot(a, b, preferred_element_type=F32)


def tdot(a, b):
    return lax.dot_general(a, b, NT, preferred_element_type=F32)


def turn_kernel(k_ref, v_ref, cos_ref, sin_ref, own_ref):
    x = k_ref[...].astype(F32)
    own_ref[0, 0] = (x * cos_ref[...] + pltpu.roll(x, HD // 2, 1) * sin_ref[...]).astype(BF16)
    own_ref[0, 1] = v_ref[...]


def turn(keys, values, cosf, sinf):
    whole = lambda *shape: pl.BlockSpec(shape, lambda i, *_: (0,) * len(shape))
    return pl.pallas_call(
        turn_kernel,
        out_shape=jax.ShapeDtypeStruct((1, 2, TOK, HD), BF16),
        grid=(1,),
        in_specs=[whole(TOK, HD)] * 4,
        out_specs=whole(1, 2, TOK, HD),
        compiler_params=pltpu.CompilerParams(dimension_semantics=("arbitrary",), vmem_limit_bytes=46 << 20),
        cost_estimate=pl.CostEstimate(flops=500_000, bytes_accessed=1_000_000, transcendentals=0),
        name="turn",
    )(keys, values, cosf, sinf)


def load_pair(place, refs, pair):
    for n, ref in enumerate(refs):

        @pl.when(place == n)
        def _():
            pair[...] = ref[0]


def forward_kernel(
    info, qr_ref, r0, r2, r1, r3, eg_ref, at_ref, li_ref, pt_ref, acc, pair
):
    step = pl.program_id(0)

    @pl.when(step == 0)
    def _():
        acc[...] = jnp.zeros_like(acc)

    def one(u, _):
        slot = step * PACK + u
        flag = flag_of(info, slot)

        @pl.when(flag > 0)
        def _():
            load_pair(place_of(info, slot), (r0, r2, r1, r3), pair)

        def body(mode):
            key = pair[0]
            value = jnp.concatenate([pair[1], jnp.ones((TOK, HD), BF16)], axis=1)
            rows = HALF
            for h in range(2):
                for part in range(TOK // rows):
                    at = pl.ds(part * rows, rows)
                    s = tdot(qr_ref[at, h * HD : (h + 1) * HD], key)
                    th = jnp.tanh(s * (QUERY_MULTIPLIER / SOFT_CAP))
                    ex = jnp.exp2(th * (SOFT_CAP * LOG2E))
                    if mode:
                        t = lax.broadcasted_iota(jnp.int32, (rows, TOK), 0) + part * rows
                        k = lax.broadcasted_iota(jnp.int32, (rows, TOK), 1)
                        ex = jnp.where(k > t if mode == 1 else k <= t, ex, 0.0)
                    eb = ex.astype(BF16)
                    eg_ref[u, 0, h, at, :] = eb
                    eg_ref[u, 1, h, at, :] = (ex * (1.0 - th * th)).astype(BF16)
                    acc[h, at, :] += ndot(eb, value)

        for want, mode in ((1, 1), (2, 2), (3, 0)):

            @pl.when(flag == want)
            def _():
                body(mode)

        return 0

    lax.fori_loop(0, PACK, one, 0)

    @pl.when(step == SLOTS // PACK - 1)
    def _():
        for h in range(2):
            inverse = 1.0 / acc[h, :, HD:]
            at_ref[:, h * HD : (h + 1) * HD] = (acc[h, :, :HD] * inverse).astype(BF16)
            li_ref[:, h * HD : (h + 1) * HD] = inverse
        row = lax.broadcasted_iota(jnp.int32, (2 * HD, 2 * HD), 0)
        col = lax.broadcasted_iota(jnp.int32, (2 * HD, 2 * HD), 1)
        core, left, plane, four, head = row // 128, (row // 64) % 2, (row // 8) % 8, (row // 2) % 4, row % 2
        source = head * HD + plane * 16 + left * 8 + core * 4 + four
        pick = jnp.where(col == source, 1.0, 0.0).astype(BF16)
        pt_ref[...] = tdot(pick, at_ref[...]).astype(BF16)


def spin_kernel(q_ref, cos_ref, sin_ref, qr_ref):
    for h in range(2):
        col = slice(h * HD, (h + 1) * HD)
        x = q_ref[:, col].astype(F32)
        qr_ref[:, col] = (x * cos_ref[...] + pltpu.roll(x, HD // 2, 1) * sin_ref[...]).astype(BF16)


def spin(queries, cosf, sinf):
    whole = lambda *shape: pl.BlockSpec(shape, lambda i, *_: (0,) * len(shape))
    return pl.pallas_call(
        spin_kernel,
        out_shape=jax.ShapeDtypeStruct((TOK, 2 * HD), BF16),
        grid=(1,),
        in_specs=[whole(TOK, 2 * HD), whole(TOK, HD), whole(TOK, HD)],
        out_specs=whole(TOK, 2 * HD),
        compiler_params=pltpu.CompilerParams(dimension_semantics=("arbitrary",), vmem_limit_bytes=60 << 20),
        cost_estimate=pl.CostEstimate(flops=500_000, bytes_accessed=1_000_000, transcendentals=0),
        name="spin",
    )(queries, cosf, sinf)


def forward(info, qr, panels):
    whole = lambda *shape: pl.BlockSpec(shape, lambda i, *_: (0,) * len(shape))
    sds = jax.ShapeDtypeStruct
    eg = pl.BlockSpec((PACK, 2, 2, TOK, TOK), lambda i, f: (i, 0, 0, 0, 0))
    return pl.pallas_call(
        forward_kernel,
        out_shape=(
            sds((SLOTS, 2, 2, TOK, TOK), BF16),
            sds((TOK, 2 * HD), BF16),
            sds((TOK, 2 * HD), F32),
            sds((2 * HD, TOK), BF16),
        ),
        grid_spec=pltpu.PrefetchScalarGridSpec(
            num_scalar_prefetch=1,
            grid=(SLOTS // PACK,),
            in_specs=[
                whole(TOK, 2 * HD),
                *([pl.BlockSpec((1, 2, TOK, HD), lambda i, f: (i // (4 // PACK), 0, 0, 0))] * 4),
            ],
            out_specs=(
                eg,
                whole(TOK, 2 * HD),
                whole(TOK, 2 * HD),
                whole(2 * HD, TOK),
            ),
            scratch_shapes=[pltpu.VMEM((2, TOK, 2 * HD), F32), pltpu.VMEM((2, TOK, HD), BF16)],
        ),
        compiler_params=pltpu.CompilerParams(dimension_semantics=("arbitrary",), vmem_limit_bytes=46 << 20),
        cost_estimate=pl.CostEstimate(flops=10_000_000_000, bytes_accessed=24_000_000, transcendentals=10_000_000),
        name="attend",
    )(info, qr, *panels)


CARRY = (
    ((HALF, 2 * HD), BF16),
    ((2, HALF, HD), F32),
    ((2, HD, HALF), BF16),
    ((2, HD, HALF), BF16),
    ((2, HALF, HD), F32),
)


def stack_rows(info, cots, first, cs):
    for d, ref in enumerate(cots):
        row = pl.multiple_of(first + lax.rem(info[2] + d, 4) * 64, 64)
        cs[pl.ds(row, 64), :] = ref[...]


def prepare(full, q_ref, at_ref, li_ref, do, dl, qt, dt):
    do[...] = full.astype(BF16)
    for h in range(2):
        col = slice(h * HD, (h + 1) * HD)
        grad = full[:, col].astype(BF16).astype(F32)
        inverse = li_ref[:, col]
        total = jnp.sum(grad * at_ref[:, col].astype(F32), axis=1, keepdims=True)
        dl[h] = jnp.broadcast_to(total, (HALF, HD))
        dt[h] = (grad * inverse).T.astype(BF16)
        qt[h] = (q_ref[:, col].astype(F32) * (inverse * QUERY_MULTIPLIER)).T.astype(BF16)


def backward_kernel(base, count, has_cots, has_prev, final, info, *refs):
    refs = list(refs)
    take = lambda n: [refs.pop(0) for _ in range(n)]
    cots = take(5) if has_cots else []
    carry_in = [] if has_cots else take(4 if base == 0 else 5)
    q_ref, at_ref = take(2) if has_cots else (None, None)
    li_ref = take(1)[0] if has_cots or final else None
    cos_ref, sin_ref = take(2) if final else (None, None)
    pairs = take(4)
    (eg_ref,) = take(1)
    if has_prev:
        (prev_ref,) = take(1)
        if final:
            take(1)
        keep_ref, send_ref = take(2)
    else:
        (part_ref,) = take(1)
    qg_ref = take(1)[0] if final else None
    carry_out = [] if final else take(1)
    cs, do, dl, qt, dt, dq, pair = refs
    if not has_cots:
        do, dl, qt, dt = carry_in[:4]
    step = pl.program_id(0)

    @pl.when(step == 0)
    def _():
        if has_cots:
            stack_rows(info, cots[:4], 0, cs)
            prepare(tdot(cs[...], cots[4][...]), q_ref, at_ref, li_ref, do, dl, qt, dt)
        if base == 0:
            dq[...] = jnp.zeros_like(dq)
        else:
            dq[...] = carry_in[4][...]

    def one(u, _):
        slot = base + step * PACK + u
        place = place_of(info, slot)
        flag = flag_of(info, slot)

        def put(dk, dv):
            if not has_prev:
                part_ref[u, 0] = dk
                part_ref[u, 1] = dv
                return

            @pl.when(place < 2)
            def _():
                keep_ref[place, 0] = dk
                keep_ref[place, 1] = dv

            @pl.when(place >= 2)
            def _():
                send_ref[place - 2, 0] = dk
                send_ref[place - 2, 1] = dv

        @pl.when(flag > 0)
        def _():
            load_pair(place, pairs, pair)
            key = pair[0]
            value = pair[1]
            dk = jnp.zeros((HD, TOK), F32)
            dv = jnp.zeros((HD, TOK), F32)
            for h in range(2):
                dp = tdot(do[:, h * HD : (h + 1) * HD], value)
                x = (eg_ref[u, 1, h].astype(F32) * (dp - dl[h][:, :1])).astype(BF16)
                dq[h] += ndot(x, key)
                dk += ndot(qt[h], x)
                dv += ndot(dt[h], eg_ref[u, 0, h])
            if has_prev:
                dk = dk + prev_ref[u, 0].astype(F32)
                dv = dv + prev_ref[u, 1].astype(F32)
            put(dk.astype(BF16), dv.astype(BF16))

        if has_prev:

            @pl.when(flag == 0)
            def _():
                zero = jnp.zeros((HD, TOK), BF16)
                put(zero, zero)

        return 0

    lax.fori_loop(0, PACK, one, 0)

    @pl.when(step == count // PACK - 1)
    def _():
        if final:
            cosine = cos_ref[...]
            sine = sin_ref[...]
            for h in range(2):
                col = slice(h * HD, (h + 1) * HD)
                g = dq[h] * (li_ref[:, col] * QUERY_MULTIPLIER)
                qg_ref[:, col] = g * cosine - pltpu.roll(g, HD // 2, 1) * sine
        else:
            carry_out[0][...] = dq[...]


def backward(base, count, which, info, rows, panels, eg_all, cots=None, w2=None, carry=None, prev=None, grad=None):
    has_cots, has_prev = cots is not None, prev is not None
    final = base + count == SLOTS
    sds = jax.ShapeDtypeStruct
    whole = lambda *shape: pl.BlockSpec(shape, lambda i, *_: (0,) * len(shape))
    tok = lambda width: pl.BlockSpec((HALF, width), lambda i, f: (half_of(f, which), 0))
    eg = pl.BlockSpec((PACK, 2, 2, HALF, TOK), lambda i, f: (base // PACK + i, 0, 0, half_of(f, which), 0))
    part = pl.BlockSpec((PACK, 2, HD, TOK), lambda i, f: (base // PACK + i, 0, 0, 0))
    ins, args, alias = [], [], {}
    if has_cots:
        ins += [whole(64, 4608)] * 4 + [whole(2 * HD, 4608)]
        args += [*cots, w2]
    else:
        ins += [whole(*shape) for shape, _ in CARRY[: len(carry)]]
        args += list(carry)
    wanted = [has_cots, has_cots, has_cots or final, final, final]
    widths = [2 * HD, 2 * HD, 2 * HD, HD, HD]
    ins += [tok(n) for n, use in zip(widths, wanted) if use]
    args += [a for a, use in zip(rows, wanted) if use]
    ins += [pl.BlockSpec((1, 2, TOK, HD), lambda i, f: (base // 4 + i // (4 // PACK), 0, 0, 0))] * 4 + [eg]
    args += [*panels, eg_all]
    if has_prev:
        ins += [part]
        args += [prev]
        outs = [whole(2, 2, HD, TOK)] * 2
        shapes = [sds((2, 2, HD, TOK), BF16)] * 2
    else:
        outs = [part]
        shapes = [sds((SLOTS, 2, HD, TOK), BF16)]
    if final:
        if grad is not None:
            ins += [pl.BlockSpec(memory_space=pl.ANY)]
            args += [grad]
            alias = {len(args): len(outs)}
        outs += [tok(2 * HD)]
        shapes += [sds((TOK, 2 * HD), F32)]
    else:
        outs += [whole(*CARRY[4][0])]
        shapes += [sds(*CARRY[4])]

    def kernel(*refs):
        backward_kernel(base, count, has_cots, has_prev, final, *refs)

    return pl.pallas_call(
        kernel,
        out_shape=shapes,
        grid_spec=pltpu.PrefetchScalarGridSpec(
            num_scalar_prefetch=1,
            grid=(count // PACK,),
            in_specs=ins,
            out_specs=outs,
            scratch_shapes=[
                pltpu.VMEM((HALF, 4608) if has_cots else (16, 128), BF16),
                *(pltpu.VMEM(*c) for c in CARRY),
                pltpu.VMEM((2, TOK, HD), BF16),
            ],
        ),
        compiler_params=pltpu.CompilerParams(dimension_semantics=("arbitrary",), vmem_limit_bytes=(60 if has_prev else 46) << 20),
        input_output_aliases=alias,
        cost_estimate=pl.CostEstimate(flops=700_000_000 * count, bytes_accessed=2_000_000 * count, transcendentals=0),
    )(info, *args)


def weight_kernel(info, *refs):
    cots = refs[:8]
    pt_ref, w_ref, q_ref, at_ref, li_ref, keep_ref, send_ref, do, dl, qt, dt, cs, full = refs[8:]
    own, core = info[3], info[4]
    near = pl.multiple_of(own * HALF, HALF)
    away = pl.multiple_of((1 - own) * HALF, HALF)
    stack_rows(info, cots[:4], near, cs)
    stack_rows(info, cots[4:], away, cs)
    rows = cs[...]
    mine = pl.multiple_of(core * HD, HD)
    other = pl.multiple_of((1 - core) * HD, HD)
    both = ndot(jnp.concatenate([pt_ref[pl.ds(mine, HD), :], pt_ref[pl.ds(other, HD), :]]), rows)
    keep_ref[...] = both[:HD]
    send_ref[...] = both[HD:].astype(BF16)
    part = tdot(cs[pl.ds(away, HALF), :], w_ref[...])

    @pl.when(pl.program_id(0) == 0)
    def _():
        full[...] = part

    @pl.when(pl.program_id(0) > 0)
    def _():
        full[...] += part

    @pl.when(pl.program_id(0) == pl.num_programs(0) - 1)
    def _():
        prepare(full[...], q_ref, at_ref, li_ref, do, dl, qt, dt)


def weight(info, cots, attn_t, w2, rows):
    chunk = 2304
    sds = jax.ShapeDtypeStruct
    block = lambda n: pl.BlockSpec((n, chunk), lambda i, f: (0, i))
    whole = lambda *shape: pl.BlockSpec(shape, lambda i, *_: (0,) * len(shape))
    tok = pl.BlockSpec((HALF, 2 * HD), lambda i, f: (1 - f[3], 0))
    return pl.pallas_call(
        weight_kernel,
        out_shape=(sds((HD, 4608), F32), sds((HD, 4608), BF16), *(sds(*c) for c in CARRY[:4])),
        grid_spec=pltpu.PrefetchScalarGridSpec(
            num_scalar_prefetch=1,
            grid=(4608 // chunk,),
            in_specs=[block(64)] * 8 + [whole(2 * HD, TOK), block(2 * HD), tok, tok, tok],
            out_specs=(block(HD), block(HD), *(whole(*shape) for shape, _ in CARRY[:4])),
            scratch_shapes=[pltpu.VMEM((TOK, chunk), BF16), pltpu.VMEM((HALF, 2 * HD), F32)],
        ),
        compiler_params=pltpu.CompilerParams(dimension_semantics=("arbitrary",), vmem_limit_bytes=60 << 20),
        cost_estimate=pl.CostEstimate(flops=1_900_000_000, bytes_accessed=11_000_000, transcendentals=0),
        name="weigh",
    )(info, *cots, attn_t, w2, *rows[:3])


def settle_kernel(keep_ref, got_ref, left_ref, down_ref, cos_ref, sin_ref, kg_ref, vg_ref):
    both = keep_ref[0].astype(F32) + got_ref[0].astype(F32) + left_ref[...].astype(F32) + down_ref[...].astype(F32)
    g = both[0].T
    kg_ref[...] = g * cos_ref[...] - pltpu.roll(g, HD // 2, 1) * sin_ref[...]
    vg_ref[...] = both[1].T


def settle(keep, got, left, down, cosf, sinf):
    whole = lambda *shape: pl.BlockSpec(shape, lambda i, *_: (0,) * len(shape))
    sds = jax.ShapeDtypeStruct
    return pl.pallas_call(
        settle_kernel,
        out_shape=(sds((TOK, HD), F32), sds((TOK, HD), F32)),
        grid=(1,),
        in_specs=[whole(1, 2, HD, TOK)] * 2 + [whole(2, HD, TOK)] * 2 + [whole(TOK, HD)] * 2,
        out_specs=(whole(TOK, HD), whole(TOK, HD)),
        compiler_params=pltpu.CompilerParams(dimension_semantics=("arbitrary",), vmem_limit_bytes=46 << 20),
        cost_estimate=pl.CostEstimate(flops=500_000, bytes_accessed=2_000_000, transcendentals=0),
        name="settle",
    )(keep, got, left, down, cosf, sinf)


def local(queries, keys, values, out_weight, cotangent):
    z, xl, c = (lax.axis_index(a) for a in CTX)
    xh, y = (lax.axis_index(a) for a in HEAD)
    lane = xl * 2 + c
    ctx = z * 4 + lane
    cosf, sinf = tables(ctx * TOK)

    info = jnp.stack([lane, ctx, y, xh, c]).astype(jnp.int32)

    own = turn(keys, values, cosf, sinf)
    behind1 = along_z(own, 1)
    behind2 = along_z(own, 2)
    across0 = swap(own, "xl")
    near1 = from_y(cotangent, 1)
    near3 = from_y(cotangent, 3)
    far0 = swap(cotangent, "xh")
    near2 = from_y(cotangent, 2)
    near = [cotangent, near1, near2, near3]
    far = [far0]
    for d in (1, 2, 3):
        far.append(from_y(far0, d))
    back = jnp.concatenate([behind2, behind1])
    across = swap(back, "xl")
    mine = jnp.concatenate([back, own])
    partner1 = swap(mine, "c")
    across = jnp.concatenate([across, across0])
    partner2 = swap(across, "c")
    panels = (mine, across, partner1, partner2)

    w2 = jnp.transpose(out_weight, (1, 0, 2)).reshape(2 * HD, 4608)

    qr = spin(queries, cosf, sinf)
    eg, attn, linv, attn_t = forward(info, qr, panels)
    rows = (qr, attn, linv, cosf, sinf)
    prev, half = backward(0, SLOTS, 1, info, rows, panels, eg, cots=near, w2=w2)

    wkeep, wsend, *carry = weight(info, near + far, attn_t, w2, rows)
    wgot = swap(wsend, "c")
    wkeep, wgot = wkeep.reshape(2, 64, 4608), wgot.reshape(2, 64, 4608)
    half_at = lambda a, n: lax.dynamic_index_in_dim(a, n, 0, False).astype(F32)
    wgive = (half_at(wkeep, 1 - xl) + half_at(wgot, 1 - xl)).astype(BF16)
    wback = swap(wgive, "xl")
    wz = (half_at(wkeep, xl) + half_at(wgot, xl) + wback.astype(F32)).astype(BF16).reshape(8, 8, 4608)
    wz = lax.all_to_all(wz, "z", 0, 0, tiled=True)
    weight_grad = jnp.sum(wz.astype(F32), axis=0).reshape(4, 2, 4608)

    total = []
    for p in range(PANELS):
        out = backward(
            p * 4, 4, 2, info, rows, panels, eg,
            carry=carry, prev=prev, grad=half if p == PANELS - 1 else None,
        )
        keep, send, last = out
        carry = [*carry[:4], last]
        got = swap(send, "c")
        give = (keep[1].astype(F32) + got[1].astype(F32)).astype(BF16)
        turned = swap(give, "xl")
        total.append((keep, got, turned))
    wide = lambda keep, got, turned: keep[0].astype(F32) + got[0].astype(F32) + turned.astype(F32)
    query_grad = last
    down1 = along_z(wide(*total[0]).astype(BF16), -1)
    down0 = along_z((wide(*total[1]) + down1.astype(F32)).astype(BF16), -1)
    key_grad, value_grad = settle(*total[2], down0, cosf, sinf)
    return query_grad, key_grad, value_grad, weight_grad


def solution(mesh):
    fine = Mesh(mesh.devices.reshape(8, 2, 2, 2, 4), CTX + HEAD)
    placed = (P(CTX, HEAD), P(CTX, HEAD), P(CTX, HEAD), P(None, HEAD, None), P(CTX + HEAD, None))
    return jax.shard_map(
        local,
        mesh=fine,
        in_specs=placed,
        out_specs=(P(CTX, HEAD), P(CTX, HEAD), P(CTX, HEAD), P(CTX, HEAD, None)),
        check_vma=False,
    )
```
